256 devices in a mesh: seq: 32 (over y, z), head: 8 (over x, core).
Axes of the slice: x: 4, y: 4, z: 8, core: 2. Of those that a mesh axis runs over, the one named last changes fastest.
Arguments:
- tokens: bfloat16 [16384, 2048], P('seq'), may hold values from -24 to 24
- w_query: bfloat16 [2048, 2048], P(None, 'head'), may hold values from -0.125 to 0.125
- w_key: bfloat16 [2048, 2048], P(None, 'head'), may hold values from -0.125 to 0.125
- w_value: bfloat16 [2048, 2048], P(None, 'head'), may hold values from -0.125 to 0.125
- w_out: bfloat16 [2048, 2048], P('head'), may hold values from -0.125 to 0.125
- shared_gate: bfloat16 [2048, 1024], P(None, 'head'), may hold values from -0.125 to 0.125
- shared_up: bfloat16 [2048, 1024], P(None, 'head'), may hold values from -0.125 to 0.125
- shared_down: bfloat16 [1024, 2048], P('head'), may hold values from -0.1875 to 0.1875
- expert_gate: bfloat16 [64, 2048, 1024], P('seq', None, 'head'), may hold values from -0.125 to 0.125
- expert_up: bfloat16 [64, 2048, 1024], P('seq', None, 'head'), may hold values from -0.125 to 0.125
- expert_down: bfloat16 [64, 1024, 2048], P('seq', 'head'), may hold values from -0.1875 to 0.1875
- expert_ids: int32 [16384, 1], P('seq'), may hold values from 0 to 63; in each aligned block of 512 rows (0 to 511, 512 to 1023, ...) at most 16 rows name the same one
Outputs:
- output: bfloat16 [16384, 2048], P('seq', 'head')
The draws below stay inside these ranges and needn't reach their ends.
Inputs may be any that keep to these rules, and one draw needn't show every extreme that they name: `expert_ids`: among the 512 tokens of one index of seq (aligned blocks of the sequence) at most 16 name the same expert, and in some block of every draw one expert is named by exactly 16 tokens.
All inputs are finite; a program needn't handle non-finite values.
Results may differ from the reference program's by a relative error of at most 0.015.
Values may be sent and summed in bfloat16 or wider, within the bound.
A program may use at most 128 MiB of HBM per device.

```python
import math
import jax
import jax.numpy as jnp
import numpy as np
from jax import lax

D = 2048
H = 16
HD = 128
SH = 1024
FF = 1024
EXPERTS = 64
TOK_DEV = 512
CAP = 16
TOKENS = 16384
N_SEQ = 32
N_HEAD = 8


def draw_tokens(key, part):
    column_key, row_key, value_key, common_key = jax.random.split(jax.random.fold_in(key, 17), 4)
    columns = jnp.arange(D, dtype=jnp.float32) / D
    column_scale = 0.12 * jnp.exp(columns * math.log(5.0) + jax.random.uniform(column_key, (D,), jnp.float32, 0.0, math.log(2.0)))
    block_count = TOKENS // TOK_DEV
    row_scale = jnp.exp(jax.random.uniform(row_key, (TOKENS, 1), jnp.float32, 0.0, math.log(2.0)))
    values = jnp.clip(jax.random.normal(value_key, (TOKENS, D), jnp.float32), -3.0, 3.0)
    common = jnp.clip(jax.random.normal(common_key, (block_count, 1, D), jnp.float32), -3.0, 3.0)
    values = (values.reshape(block_count, TOK_DEV, D) + common).reshape(TOKENS, D)
    return (values * row_scale * column_scale[None, :]).astype(jnp.bfloat16)


def levels(key, shape, cuts, smallest, largest):
    def one(axis_at, blocks):
        draws = jax.random.uniform(jax.random.fold_in(jax.random.fold_in(key, 6), axis_at), (blocks,), jnp.float32, smallest / len(cuts), largest / len(cuts))
        return jnp.repeat(jnp.exp(draws), shape[axis_at] // blocks).reshape((-1,) + (1,) * (len(shape) - axis_at - 1))

    level = one(*cuts[0])
    for cut in cuts[1:]:
        level = level * one(*cut)
    return level


def deal_out(stream_key, own, number, rows, amount, top, limit, lean):
    ranking = jax.random.permutation(stream_key, amount)
    crowded, usual = portions_of(amount, rows * top, limit, lean, True), portions_of(amount, rows * top, limit, lean, False)
    places = jnp.arange(amount)

    def named(tallies, offset_by):
        used = int((tallies > 0).sum())
        fixed = max(1, used // 4)
        passed = fixed + (places - fixed + offset_by * (used - fixed)) % max(1, amount - fixed)
        return jnp.zeros((amount,), jnp.int32).at[ranking[jnp.where(places < fixed, places, passed)]].set(jnp.asarray(tallies, jnp.int32))

    tallies = jnp.where(number % 4 == 0, named(crowded, number // 4), named(usual, number - number // 4 - 1))
    mixed = jax.random.permutation(jax.random.fold_in(own, 3), amount)
    source_of, taker = mixed[0:amount // 2 * 2:2], mixed[1:amount // 2 * 2:2]
    room = jnp.minimum(tallies[source_of] - 1, limit - tallies[taker]) // 2
    room = jnp.where((source_of == ranking[0]) | (taker == ranking[0]) | (tallies[taker] == 0), 0, jnp.maximum(room, 0))
    passed = jax.random.randint(jax.random.fold_in(own, 4), (amount // 2,), 0, 1 << 20) % (room + 1)
    tallies = tallies.at[source_of].add(-passed).at[taker].add(passed)
    members = jnp.searchsorted(jnp.cumsum(tallies), jnp.arange(rows * top), side="right").astype(jnp.int32)
    grid = members.reshape(top, rows).T
    grid = grid[jax.random.permutation(jax.random.fold_in(own, 1), rows)]
    offset_by = jax.random.randint(jax.random.fold_in(own, 2), (rows, 1), 0, top)
    return jnp.take_along_axis(grid, (jnp.arange(top)[None, :] + offset_by) % top, axis=1)


def portions_of(count, total, most, skew, full):
    portions = [(1 << 20) // math.isqrt(grade ** skew) + 1 for grade in range(1, count + 1)]
    largest = most if full else min(most, max(-(-total // count), total * portions[0] // sum(portions)))
    least = 1 if total - largest >= count - 1 else 0
    given, rest = [largest] + [least] * (count - 1), total - largest - least * (count - 1)
    while rest > 0:
        movable = [i for i in range(1, count) if given[i] < largest] or [i for i in range(1, count) if given[i] < most]
        whole, left = sum([portions[i] for i in movable]), rest
        for i in movable:
            addition = min(most - given[i], max(1, left * portions[i] // whole), rest)
            given[i] = given[i] + addition
            rest = rest - addition
    return np.array(given)


def bell_draw(stream_key, extent, spread, bound, shards=(), kind=jnp.bfloat16):
    factor_of = levels(stream_key, extent, shards, -0.22, 0.18) if shards else 1.0
    values = jax.random.normal(stream_key, extent, jnp.float32) * spread * factor_of
    return jnp.minimum(jnp.maximum(values, -bound), bound).astype(kind)


def setup_inputs(seed: int = 0) -> dict:
    splits = jax.random.split(jax.random.key(seed), 13)
    tokens = draw_tokens(jax.random.fold_in(splits[12], 71), 0)
    w_query = bell_draw(splits[1], (D, H * HD), D ** -0.5, 0.125, ((1, 8),))
    w_key = bell_draw(splits[2], (D, H * HD), D ** -0.5, 0.125, ((1, 8),))
    w_value = bell_draw(splits[3], (D, H * HD), D ** -0.5, 0.125, ((1, 8),))
    w_out = bell_draw(splits[4], (H * HD, D), (H * HD) ** -0.5, 0.125, ((0, 8),))
    shared_gate = bell_draw(splits[5], (D, SH), D ** -0.5, 0.125, ((1, 8),))
    shared_up = bell_draw(splits[6], (D, SH), D ** -0.5, 0.125, ((1, 8),))
    shared_down = bell_draw(splits[7], (SH, D), SH ** -0.5, 0.1875, ((0, 8),))
    expert_gate = bell_draw(splits[8], (EXPERTS, D, FF), D ** -0.5, 0.125, ((0, 32), (2, 8)))
    expert_up = bell_draw(splits[9], (EXPERTS, D, FF), D ** -0.5, 0.125, ((0, 32), (2, 8)))
    expert_down = bell_draw(splits[10], (EXPERTS, FF, D), FF ** -0.5, 0.1875, ((0, 32), (1, 8)))
    expert_ids_keys = jax.random.split(jax.random.fold_in(splits[11], 1), TOKENS // TOK_DEV)
    expert_ids_turns = jax.random.permutation(jax.random.fold_in(splits[11], 3), TOKENS // TOK_DEV)
    expert_ids = jax.vmap(lambda own, number: deal_out(jax.random.fold_in(splits[11], 2), own, number, TOK_DEV, EXPERTS, 1, CAP, 2))(expert_ids_keys, expert_ids_turns).reshape((TOKENS, 1))
    return {"tokens": tokens, "w_query": w_query, "w_key": w_key, "w_value": w_value, "w_out": w_out, "shared_gate": shared_gate, "shared_up": shared_up, "shared_down": shared_down, "expert_gate": expert_gate, "expert_up": expert_up, "expert_down": expert_down, "expert_ids": expert_ids}


def rms_rows(values):
    return values * lax.rsqrt(lax.optimization_barrier(jnp.mean(values * values, axis=-1, keepdims=True)) + 1e-06)

def reference(tokens, w_query, w_key, w_value, w_out, shared_gate, shared_up, shared_down, expert_gate, expert_up, expert_down, expert_ids):
    highest = lax.Precision.HIGHEST
    inputs = tokens.astype(jnp.float32)
    normed_input = rms_rows(inputs).astype(jnp.bfloat16)
    query_rows = jnp.dot(normed_input, w_query, preferred_element_type=jnp.float32).astype(jnp.bfloat16)
    key_rows = jnp.dot(normed_input, w_key, preferred_element_type=jnp.float32).astype(jnp.bfloat16)
    value_rows = jnp.dot(normed_input, w_value, preferred_element_type=jnp.float32).astype(jnp.bfloat16)
    block_count = TOKENS // TOK_DEV

    def split_blocks(array):
        return array.astype(jnp.float32).reshape(block_count, TOK_DEV, H, HD)
    causal = jnp.arange(TOK_DEV)[:, None] >= jnp.arange(TOK_DEV)[None, :]

    def advance(states, block_in):
        query_block, key_block, value_block = block_in
        scores = jnp.einsum('thd,shd->hts', query_block, key_block, precision=highest)
        scores = jnp.where(causal[None], scores, 0.0)
        within = jnp.einsum('hts,shd->thd', scores, value_block, precision=highest)
        before = jnp.einsum('thd,hde->the', query_block, states, precision=highest)
        states = states + jnp.einsum('thd,the->hde', key_block, value_block, precision=highest)
        return (states, within + before)
    _, attended = lax.scan(advance, jnp.zeros((H, HD, HD), jnp.float32), (split_blocks(query_rows), split_blocks(key_rows), split_blocks(value_rows)))
    attended = attended.reshape(TOKENS, H, HD)
    head_normed = rms_rows(attended).reshape(TOKENS, H * HD).astype(jnp.bfloat16)
    group_cols = H * HD // N_HEAD
    attn_sum = jnp.zeros((TOKENS, D), jnp.float32)
    for group in range(N_HEAD):
        head_term = jnp.dot(head_normed[:, group * group_cols:(group + 1) * group_cols], w_out[group * group_cols:(group + 1) * group_cols], preferred_element_type=jnp.float32).astype(jnp.bfloat16)
        attn_sum = attn_sum + lax.optimization_barrier(head_term).astype(jnp.float32)
    residual = inputs + attn_sum
    normed_mid = rms_rows(residual).astype(jnp.bfloat16)
    shared_hidden = (jax.nn.silu(jnp.dot(normed_mid, shared_gate, preferred_element_type=jnp.float32)) * jnp.dot(normed_mid, shared_up, preferred_element_type=jnp.float32)).astype(jnp.bfloat16)
    expert_of = expert_ids[:, 0].astype(jnp.int32)
    onehot = (expert_of.reshape(N_SEQ, TOK_DEV, 1) == jnp.arange(EXPERTS, dtype=jnp.int32)[None, None, :]).astype(jnp.int32)
    slot_rank = (lax.optimization_barrier(jnp.sum(jnp.cumsum(onehot, axis=1) * onehot, axis=2)).reshape(TOKENS) - 1).astype(jnp.int32)
    block_index = (jnp.arange(TOKENS, dtype=jnp.int32) // TOK_DEV).astype(jnp.int32)
    position = (expert_of * (N_SEQ * CAP) + block_index * CAP + slot_rank).astype(jnp.int32)
    buffer_rows = EXPERTS * N_SEQ * CAP
    buffer = jnp.zeros((buffer_rows, D), jnp.bfloat16).at[position].set(normed_mid)
    buffer = buffer.reshape(EXPERTS, N_SEQ * CAP, D)
    routed_hidden = lax.map(lambda operands: (jax.nn.silu(jnp.dot(operands[0], operands[1], preferred_element_type=jnp.float32)) * jnp.dot(operands[0], operands[2], preferred_element_type=jnp.float32)).astype(jnp.bfloat16), (buffer, expert_gate, expert_up))
    expert_cols = FF // N_HEAD
    shared_cols = SH // N_HEAD
    routed_sum = jnp.zeros((TOKENS, D), jnp.float32)
    shared_sum = jnp.zeros((TOKENS, D), jnp.float32)
    for group in range(N_HEAD):
        low = group * expert_cols
        routed_term = lax.map(lambda operands: jnp.dot(operands[0][:, low:low + expert_cols], operands[1][low:low + expert_cols], preferred_element_type=jnp.float32).astype(jnp.bfloat16), (routed_hidden, expert_down))
        routed_term = routed_term.reshape(buffer_rows, D)[position]
        routed_sum = routed_sum + lax.optimization_barrier(routed_term).astype(jnp.float32)
        shared_term = jnp.dot(shared_hidden[:, group * shared_cols:(group + 1) * shared_cols], shared_down[group * shared_cols:(group + 1) * shared_cols], preferred_element_type=jnp.float32).astype(jnp.bfloat16)
        shared_sum = shared_sum + lax.optimization_barrier(shared_term).astype(jnp.float32)
    routed_total = routed_sum.astype(jnp.bfloat16)
    routed_back = lax.optimization_barrier(routed_total).astype(jnp.float32)
    return (residual + shared_sum + routed_back).astype(jnp.bfloat16)
```

```python
import jax
import jax.numpy as jnp
from jax import lax
from jax.sharding import PartitionSpec as P

HD = 128
EXPERTS = 64
CAP = 16
F32 = jnp.float32
BF16 = jnp.bfloat16


def dot(a, b):
    return jnp.dot(a, b, preferred_element_type=F32)


def two_part(values):
    high = values.astype(BF16)
    return high, (values - high.astype(F32)).astype(BF16)


def head_columns(weights):
    return lax.all_to_all(weights, "head", split_axis=1, concat_axis=0, tiled=True)


def gather_columns(block):
    return lax.all_gather(block, "head", axis=1, tiled=True)


def carried_state(local_state):
    shape = local_state.shape
    length = lax.axis_size("seq")
    chunks = local_state.reshape(length, -1, HD)
    mine = lax.all_to_all(chunks, "seq", split_axis=0, concat_axis=0, tiled=True)
    earlier = jnp.arange(length)[:, None] > jnp.arange(length)[None, :]
    before = jnp.sum(jnp.where(earlier[:, :, None, None], mine[None], 0.0), axis=1)
    back = lax.all_to_all(before, "seq", split_axis=0, concat_axis=0, tiled=True)
    return back.reshape(shape)


def row_scale(rows):
    wide = rows.astype(F32)
    return lax.rsqrt(jnp.mean(wide * wide, axis=-1, keepdims=True) + 1e-06)


def shards(
    tokens,
    w_query,
    w_key,
    w_value,
    w_out,
    shared_gate,
    shared_up,
    shared_down,
    expert_gate,
    expert_up,
    expert_down,
    expert_ids,
):
    rows, width = tokens.shape
    heads = w_query.shape[1] // HD
    owned = expert_gate.shape[0]
    sources = lax.axis_size("seq")
    experts = owned * sources
    cols = width // lax.axis_size("head")
    head = lax.axis_index("head")

    out_cols = head_columns(w_out)
    shared_cols = head_columns(shared_down)
    expert_cols = lax.all_to_all(expert_down, "head", split_axis=2, concat_axis=1, tiled=True)

    inputs = tokens.astype(F32)
    normed = (inputs * row_scale(tokens)).astype(BF16)
    query = dot(normed, w_query).astype(BF16).reshape(rows, heads, HD)
    key = dot(normed, w_key).astype(BF16).reshape(rows, heads, HD)
    value = dot(normed, w_value).astype(BF16).reshape(rows, heads, HD)
    state = jnp.einsum("thd,the->hde", key, value, preferred_element_type=F32)
    carried = carried_state(state)
    causal = jnp.arange(rows)[:, None] >= jnp.arange(rows)[None, :]
    scores = jnp.einsum("thd,shd->hts", query, key, preferred_element_type=F32)
    scores = two_part(jnp.where(causal[None], scores, 0.0))
    carried = two_part(carried)
    attended = sum(
        jnp.einsum("hts,shd->thd", part, value, preferred_element_type=F32) for part in scores
    ) + sum(
        jnp.einsum("thd,hde->the", query, part, preferred_element_type=F32) for part in carried
    )
    head_normed = (
        attended * lax.rsqrt(jnp.mean(attended * attended, axis=-1, keepdims=True) + 1e-06)
    ).astype(BF16).reshape(rows, heads * HD)

    own_tokens = lax.dynamic_slice_in_dim(tokens, head * cols, cols, 1)
    residual = own_tokens.astype(F32) + dot(gather_columns(head_normed), out_cols)
    sent = residual.astype(BF16)

    expert_of = expert_ids[:, 0]
    same = (expert_of[:, None] == expert_of[None, :]) & causal
    rank = jnp.sum(same.astype(jnp.int32), axis=1) - 1
    slot = expert_of * CAP + rank
    chosen = jnp.arange(experts * CAP, dtype=jnp.int32)[:, None] == slot[None, :]
    chosen = chosen.astype(BF16)
    outgoing = dot(chosen, sent).astype(BF16).reshape(sources, owned, CAP, cols)
    arrived = lax.all_to_all(outgoing, "seq", split_axis=0, concat_axis=0, tiled=True)
    arrived = arrived.transpose(1, 0, 2, 3).reshape(owned * sources * CAP, cols)
    routed_in = gather_columns(arrived)

    middle = gather_columns(sent)
    scale = row_scale(middle)
    shared_hidden = (
        jax.nn.silu(dot(middle, shared_gate) * scale) * (dot(middle, shared_up) * scale)
    ).astype(BF16)

    scale = row_scale(routed_in).reshape(owned, sources * CAP, 1)
    routed_in = routed_in.reshape(owned, sources * CAP, width)
    gate = jnp.einsum("erd,edf->erf", routed_in, expert_gate, preferred_element_type=F32)
    up = jnp.einsum("erd,edf->erf", routed_in, expert_up, preferred_element_type=F32)
    routed_hidden = (jax.nn.silu(gate * scale) * (up * scale)).astype(BF16)
    both = jnp.concatenate([shared_hidden, routed_hidden.reshape(owned * sources * CAP, -1)])
    both = gather_columns(both)
    shared_out = dot(both[:rows], shared_cols)
    routed_out = jnp.einsum(
        "erf,efd->erd",
        both[rows:].reshape(owned, sources * CAP, -1),
        expert_cols,
        preferred_element_type=F32,
    ).astype(BF16)
    routed_out = routed_out.reshape(owned, sources, CAP, cols).transpose(1, 0, 2, 3)
    returned = lax.all_to_all(routed_out, "seq", split_axis=0, concat_axis=0, tiled=True)
    returned = returned.reshape(experts * CAP, cols)
    routed = lax.dot_general(
        chosen, returned, (((0,), (0,)), ((), ())), preferred_element_type=F32
    )
    return (residual + shared_out + routed).astype(BF16)


def solution(mesh):
    return jax.shard_map(
        shards,
        mesh=mesh,
        in_specs=(
            P("seq", None),
            P(None, "head"),
            P(None, "head"),
            P(None, "head"),
            P("head", None),
            P(None, "head"),
            P(None, "head"),
            P("head", None),
            P("seq", None, "head"),
            P("seq", None, "head"),
            P("seq", "head", None),
            P("seq", None),
        ),
        out_specs=P("seq", "head"),
        check_vma=False,
    )
```

```python
import functools

import jax
import jax.numpy as jnp
from jax import lax
from jax.experimental import pallas as pl
from jax.experimental.pallas import tpu as pltpu
from jax.sharding import PartitionSpec as P

HD = 128
CAP = 16
F32 = jnp.float32
BF16 = jnp.bfloat16

STATE, CARRY, DISPATCH, RETURN = range(4)
HEADS, MIDDLE, ROUTED, SHARED_HIDDEN, ROUTED_HIDDEN = 0, 1, 2, 4, 5
GATHERS = 7


def dot(a, b, contract=((1,), (0,))):
    return lax.dot_general(a, b, (contract, ((), ())), preferred_element_type=F32)


def two_part(values):
    high = values.astype(BF16)
    return high, (values - high.astype(F32)).astype(BF16)


def rms(total, count):
    return lax.rsqrt(total * (1.0 / count) + 1e-06)


def silu(v):
    return v / (1.0 + jnp.exp(-v))


def layer_kernel(
    n_seq, n_head,
    tok, wq, wk, wv, wo, sg, su, sd, eg, eu, ed, ids_col, ids_row,
    out,
    x, own, normed, wqkv, wo_v, sd_v, ed_v, sgu, egu, qkv, st, got, pre, car, att,
    hn, mid, rin, outb, hs, hr, rout, back, res, chosen, chosen_t, acc, sq,
    load_sem, w_send, w_recv, s_send, s_recv, g_send, g_recv,
):
    rows, width = x.shape
    cols = width // n_head
    owned = eg.shape[0]
    hidden = eg.shape[2]
    span = 2 * HD
    per = n_seq // 2
    s = lax.axis_index("seq")
    h = lax.axis_index("head")
    core = h % 2
    chip = h // 2
    chips = n_head // 2
    partner = 2 * chip + 1 - core
    right = 2 * ((chip + 1) % chips) + core
    left = 2 * ((chip + chips - 1) % chips) + core
    far = 2 * ((chip + 2) % chips) + core

    def twin(b):
        return 2 * (b // 2) + 1 - b % 2

    def col_slice(index, size):
        return pl.ds(pl.multiple_of(index * size, 128), size)

    def load(i, src, dst):
        return pltpu.make_async_copy(src, dst, load_sem.at[i])

    loads = [
        load(0, tok, x),
        load(1, wq, wqkv.at[:, pl.ds(0, span)]),
        load(2, wk, wqkv.at[:, pl.ds(span, span)]),
        load(3, wv, wqkv.at[:, pl.ds(2 * span, span)]),
        load(4, tok.at[:, col_slice(h, cols)], own),
        load(5, wo.at[:, col_slice(h, cols)], wo_v.at[h]),
        load(6, sd.at[:, col_slice(h, cols)], sd_v.at[h]),
        load(7, ed.at[:, :, col_slice(h, cols)], ed_v.at[h]),
        load(8, sg, sgu.at[:, pl.ds(0, hidden)]),
        load(9, su, sgu.at[:, pl.ds(hidden, hidden)]),
        load(10, eg, egu.at[:, :, pl.ds(0, hidden)]),
        load(11, eu, egu.at[:, :, pl.ds(hidden, hidden)]),
    ]

    def seq_peer(t):
        return (s + t) % n_seq

    def head_peer(t):
        return (h + t) % n_head

    barrier = pltpu.get_barrier_semaphore()

    def greet_seq(t, carry):
        pl.semaphore_signal(barrier, inc=1, device_id={"seq": seq_peer(t)})
        return carry

    def greet_head(t, carry):
        pl.semaphore_signal(barrier, inc=1, device_id={"head": head_peer(t)})
        return carry

    lax.fori_loop(1, n_head, greet_head, 0)
    lax.fori_loop(1, n_seq, greet_seq, 0)
    for copy in loads:
        copy.start()

    def weight_copy(i, peer):
        src, dst = (
            (wo.at[:, col_slice(peer, cols)], wo_v.at[h]),
            (sd.at[:, col_slice(peer, cols)], sd_v.at[h]),
            (ed.at[:, :, col_slice(peer, cols)], ed_v.at[h]),
        )[i]
        return pltpu.make_async_remote_copy(
            src, dst, w_send.at[i, peer], w_recv.at[i, h], device_id={"head": peer}
        )

    def weight_arrival(i, source):
        dst = (wo_v, sd_v, ed_v)[i].at[source]
        return pltpu.make_async_remote_copy(
            dst, dst, w_send.at[i, source], w_recv.at[i, source], device_id={"head": source}
        )

    def seq_copy(e, peer):
        src, dst = (
            (st.at[peer], got.at[s]),
            (pre.at[peer], car.at[s]),
            (outb.at[peer], rin.at[h, :, s]),
            (rout.at[:, peer], back.at[s]),
        )[e]
        return pltpu.make_async_remote_copy(
            src, dst, s_send.at[e, peer], s_recv.at[e, s], device_id={"seq": peer}
        )

    def seq_arrival(e, source):
        dst = (got.at[source], car.at[source], rin.at[h, :, source], back.at[source])[e]
        return pltpu.make_async_remote_copy(
            dst, dst, s_send.at[e, source], s_recv.at[e, source], device_id={"seq": source}
        )

    def seq_start(e):
        def one(t, carry):
            seq_copy(e, seq_peer(t)).start()
            return carry

        lax.fori_loop(1, n_seq, one, 0)

    def seq_wait(e):
        def one(t, carry):
            seq_arrival(e, seq_peer(t)).wait_recv()
            return carry

        lax.fori_loop(1, n_seq, one, 0)

    def view(g, b):
        if g == HEADS:
            return hn.at[b]
        if g == MIDDLE:
            return mid.at[b]
        if g == SHARED_HIDDEN:
            return hs.at[b]
        if g >= ROUTED_HIDDEN:
            return hr.at[b, g - ROUTED_HIDDEN]
        return rin.at[b, g - ROUTED]

    def half(g, b, k):
        whole = view(g, b)
        n = whole.shape[0] // 2
        return whole.at[pl.ds(k * n, n)]

    def leg(g, i):
        ref, target = (
            (lambda: view(g, h), right),
            (lambda: view(g, h), left),
            (lambda: view(g, h), partner),
            (lambda: half(g, left, 0), right),
            (lambda: half(g, right, 1), left),
            (lambda: view(g, left), partner),
            (lambda: view(g, right), partner),
            (lambda: half(g, far, 0), partner),
            (lambda: half(g, far, 1), partner),
        )[i]
        ref = ref()
        return pltpu.make_async_remote_copy(
            ref, ref, g_send.at[g, i], g_recv.at[g, i], device_id={"head": target}
        )

    def leg_wait(g, i):
        ref = (
            lambda: view(g, left),
            lambda: view(g, right),
            lambda: view(g, partner),
            lambda: half(g, far, 0),
            lambda: half(g, far, 1),
            lambda: view(g, twin(left)),
            lambda: view(g, twin(right)),
            lambda: half(g, twin(far), 0),
            lambda: half(g, twin(far), 1),
        )[i]()
        pltpu.make_async_remote_copy(
            ref, ref, g_send.at[g, i], g_recv.at[g, i], device_id={"head": partner}
        ).wait_recv()

    def gather_start(g):
        for i in range(3):
            leg(g, i).start()

    def gather_pass(g):
        leg_wait(g, 0)
        leg(g, 3).start()
        leg(g, 5).start()
        leg_wait(g, 1)
        leg(g, 4).start()
        leg(g, 6).start()

    def gather_far(g):
        leg_wait(g, 3)
        leg(g, 7).start()
        leg_wait(g, 4)
        leg(g, 8).start()

    def gather_use(g, use):
        use(h)
        leg_wait(g, 2)
        use(partner)
        gather_pass(g)
        use(left)
        use(right)
        gather_far(g)
        leg_wait(g, 5)
        use(twin(left))
        leg_wait(g, 6)
        use(twin(right))
        use(far)
        leg_wait(g, 7)
        leg_wait(g, 8)
        use(twin(far))

    loads[0].wait()

    def normalize(i, carry):
        at = pl.ds(pl.multiple_of(i * 32, 32), 32)
        wide = x[at, :].astype(F32)
        scale = rms(jnp.sum(wide * wide, axis=-1, keepdims=True), width)
        normed[at, :] = (wide * scale).astype(BF16)
        return carry

    lax.fori_loop(0, rows // 32, normalize, 0)
    pl.semaphore_wait(barrier, n_head - 1 + n_seq - 1)

    for i in range(3):

        def one(t, carry):
            weight_copy(i, head_peer(t)).start()
            return carry

        lax.fori_loop(1, n_head, one, 0)
    for i in (1, 2, 3):
        loads[i].wait()
    block = min(256, rows)

    def project(i, carry):
        at = pl.ds(pl.multiple_of(i * block, block), block)
        qkv[at, :] = dot(normed[at, :], wqkv[...]).astype(BF16)
        return carry

    lax.fori_loop(0, rows // block, project, 0)

    for a in range(2):
        k = qkv[:, span + a * HD : span + (a + 1) * HD]
        v = qkv[:, 2 * span + a * HD : 2 * span + (a + 1) * HD]
        st[a * per : (a + 1) * per] = dot(k, v, ((0,), (0,))).reshape(per, -1, HD)
    seq_start(STATE)
    got[s] = st[s]

    for a in range(2):
        for i in range(rows // block):
            top, end = i * block, (i + 1) * block
            q = qkv[top:end, a * HD : (a + 1) * HD]
            k = qkv[:end, span + a * HD : span + (a + 1) * HD]
            v = qkv[:end, 2 * span + a * HD : 2 * span + (a + 1) * HD]
            scores = dot(q, k, ((1,), (1,)))
            row = lax.broadcasted_iota(jnp.int32, scores.shape, 0) + top
            col = lax.broadcasted_iota(jnp.int32, scores.shape, 1)
            high, low = two_part(jnp.where(row >= col, scores, 0.0))
            att[top:end, a * HD : (a + 1) * HD] = dot(high, v) + dot(low, v)

    def running(j, total):
        @pl.when(j != s)
        def _():
            seq_arrival(STATE, j).wait_recv()

        pre[j] = total
        return total + got[j]

    lax.fori_loop(0, n_seq, running, jnp.zeros(pre.shape[1:], F32))
    seq_start(CARRY)
    car[s] = pre[s]

    ids_c = ids_col[...]
    ids_r = ids_row[...]
    row = lax.broadcasted_iota(jnp.int32, (rows, rows), 0)
    col = lax.broadcasted_iota(jnp.int32, (rows, rows), 1)
    same = ids_c == ids_r
    rank_r = jnp.sum(jnp.where(same & (row <= col), 1.0, 0.0), axis=0, keepdims=True)
    rank_c = jnp.sum(jnp.where(same & (col <= row), 1.0, 0.0), axis=1, keepdims=True)
    base_r = ids_r.astype(F32) * CAP + rank_r - 1.0
    base_c = ids_c.astype(F32) * CAP + rank_c - 1.0
    slots = n_seq * owned * CAP
    place = lax.broadcasted_iota(jnp.int32, (slots, 1), 0).astype(F32)
    chosen[...] = jnp.where(place == base_r, 1.0, 0.0).astype(BF16)
    place = lax.broadcasted_iota(jnp.int32, (1, slots), 1).astype(F32)
    chosen_t[...] = jnp.where(place == base_c, 1.0, 0.0).astype(BF16)

    seq_wait(CARRY)
    for a in range(2):
        high, low = two_part(car[a * per : (a + 1) * per].reshape(HD, HD))
        q = qkv[:, a * HD : (a + 1) * HD]
        whole = att[:, a * HD : (a + 1) * HD] + dot(q, high) + dot(q, low)
        scale = rms(jnp.sum(whole * whole, axis=-1, keepdims=True), HD)
        hn[h, :, a * HD : (a + 1) * HD] = (whole * scale).astype(BF16)
    gather_start(HEADS)

    loads[4].wait()
    res[...] = own[...].astype(F32)
    loads[5].wait()

    def weights_wait(i):
        def one(t, carry):
            weight_arrival(i, head_peer(t)).wait_recv()
            return carry

        lax.fori_loop(1, n_head, one, 0)

    weights_wait(0)

    def use_heads(b):
        res[...] += dot(hn[b], wo_v[b])

    gather_use(HEADS, use_heads)
    mid[h] = res[...].astype(BF16)
    gather_start(MIDDLE)
    outb[...] = dot(chosen[...], mid[h]).astype(BF16).reshape(outb.shape)
    seq_start(DISPATCH)
    rin[h, :, s] = outb[s]

    loads[8].wait()
    loads[9].wait()
    acc[...] = jnp.zeros_like(acc)
    sq[...] = jnp.zeros_like(sq)

    def use_middle(b):
        part = mid[b]
        acc[pl.ds(0, rows), :] += dot(part, sgu[pl.ds(pl.multiple_of(b * cols, cols), cols), :])
        wide = part.astype(F32)
        sq[pl.ds(0, rows), :] += wide * wide

    def activate(count):
        scale = rms(jnp.sum(sq[pl.ds(0, count), :], axis=-1, keepdims=True), width)
        gate = acc[pl.ds(0, count), pl.ds(0, hidden)] * scale
        up = acc[pl.ds(0, count), pl.ds(hidden, hidden)] * scale
        return (silu(gate) * up).astype(BF16)

    gather_use(MIDDLE, use_middle)

    seq_wait(DISPATCH)
    for e in range(owned):
        gather_start(ROUTED + e)
    hs[h] = activate(rows)
    gather_start(SHARED_HIDDEN)
    loads[10].wait()
    loads[11].wait()
    taken = n_seq * CAP
    for e in range(owned):
        acc[...] = jnp.zeros_like(acc)
        sq[...] = jnp.zeros_like(sq)

        def use_routed(b):
            part = rin[b, e].reshape(taken, cols)
            acc[pl.ds(0, taken), :] += dot(part, egu[e, pl.ds(pl.multiple_of(b * cols, cols), cols), :])
            wide = part.astype(F32)
            sq[pl.ds(0, taken), :] += wide * wide

        gather_use(ROUTED + e, use_routed)
        hr[h, e] = activate(taken)
        gather_start(ROUTED_HIDDEN + e)

    loads[6].wait()
    loads[7].wait()
    weights_wait(1)
    weights_wait(2)

    def use_shared(b):
        res[...] += dot(hs[b], sd_v[b])

    gather_use(SHARED_HIDDEN, use_shared)
    for e in range(owned):
        acc[...] = jnp.zeros_like(acc)

        def use_hidden(b):
            acc[pl.ds(0, taken), pl.ds(0, cols)] += dot(hr[b, e], ed_v[b, e])

        gather_use(ROUTED_HIDDEN + e, use_hidden)
        rout[e] = acc[pl.ds(0, taken), pl.ds(0, cols)].astype(BF16).reshape(rout.shape[1:])
    seq_start(RETURN)
    back[s] = rout[:, s]
    seq_wait(RETURN)
    routed = dot(chosen_t[...], back[...].reshape(slots, cols))
    out[...] = (res[...] + routed).astype(BF16)

    def weights_left(t, carry):
        for i in range(3):
            weight_copy(i, head_peer(t)).wait_send()
        return carry

    lax.fori_loop(1, n_head, weights_left, 0)

    def seq_left(t, carry):
        for e in range(4):
            seq_copy(e, seq_peer(t)).wait_send()
        return carry

    lax.fori_loop(1, n_seq, seq_left, 0)
    for g in range(GATHERS):
        for i in range(9):
            leg(g, i).wait_send()


def shards(
    tokens,
    w_query,
    w_key,
    w_value,
    w_out,
    shared_gate,
    shared_up,
    shared_down,
    expert_gate,
    expert_up,
    expert_down,
    expert_ids,
):
    n_seq, n_head = lax.axis_size("seq"), lax.axis_size("head")
    rows, width = tokens.shape
    cols = width // n_head
    owned, _, hidden = expert_gate.shape
    heads = w_query.shape[1]
    taken = n_seq * CAP
    slots = owned * taken
    chunk = heads // n_seq
    most = max(rows, taken)
    any_spec = pl.BlockSpec(memory_space=pl.ANY)
    vmem_spec = pl.BlockSpec(memory_space=pltpu.VMEM)
    V = pltpu.VMEM
    dma = pltpu.SemaphoreType.DMA
    return pl.pallas_call(
        functools.partial(layer_kernel, n_seq, n_head),
        out_shape=jax.ShapeDtypeStruct((rows, cols), BF16),
        in_specs=[any_spec] * 11 + [vmem_spec] * 2,
        out_specs=vmem_spec,
        scratch_shapes=[
            V((rows, width), BF16),
            V((rows, cols), BF16),
            V((rows, width), BF16),
            V((width, 3 * heads), BF16),
            V((n_head, heads, cols), BF16),
            V((n_head, hidden, cols), BF16),
            V((n_head, owned, hidden, cols), BF16),
            V((width, 2 * hidden), BF16),
            V((owned, width, 2 * hidden), BF16),
            V((rows, 3 * heads), BF16),
            V((n_seq, chunk, HD), F32),
            V((n_seq, chunk, HD), F32),
            V((n_seq, chunk, HD), F32),
            V((n_seq, chunk, HD), F32),
            V((rows, heads), F32),
            V((n_head, rows, heads), BF16),
            V((n_head, rows, cols), BF16),
            V((n_head, owned, n_seq, CAP, cols), BF16),
            V((n_seq, owned, CAP, cols), BF16),
            V((n_head, rows, hidden), BF16),
            V((n_head, owned, taken, hidden), BF16),
            V((owned, n_seq, CAP, cols), BF16),
            V((n_seq, owned, CAP, cols), BF16),
            V((rows, cols), F32),
            V((slots, rows), BF16),
            V((rows, slots), BF16),
            V((most, 2 * hidden), F32),
            V((most, cols), F32),
            dma((12,)),
            dma((3, n_head)),
            dma((3, n_head)),
            dma((4, n_seq)),
            dma((4, n_seq)),
            dma((GATHERS, 9)),
            dma((GATHERS, 9)),
        ],
        compiler_params=pltpu.CompilerParams(
            collective_id=0, has_side_effects=True, vmem_limit_bytes=60 * 1024 * 1024
        ),
    )(
        tokens, w_query, w_key, w_value, w_out, shared_gate, shared_up, shared_down,
        expert_gate, expert_up, expert_down, expert_ids, expert_ids.reshape(1, rows),
    )


def solution(mesh):
    return jax.shard_map(
        shards,
        mesh=mesh,
        in_specs=(
            P("seq", None),
            P(None, "head"),
            P(None, "head"),
            P(None, "head"),
            P("head", None),
            P(None, "head"),
            P(None, "head"),
            P("head", None),
            P("seq", None, "head"),
            P("seq", None, "head"),
            P("seq", "head", None),
            P("seq", None),
        ),
        out_specs=P("seq", "head"),
        check_vma=False,
    )
```

```python
import functools

import jax
import jax.numpy as jnp
from jax import lax
from jax.experimental import pallas as pl
from jax.experimental.pallas import tpu as pltpu
from jax.sharding import PartitionSpec as P

HD = 128
CAP = 16
NY = 4
F32 = jnp.float32
BF16 = jnp.bfloat16

STATE, CARRY, DISPATCH, RETURN = 0, 1, 2, 4
EXCHANGES = 6
HEADS, MIDDLE, ROUTED, SHARED_HIDDEN, ROUTED_HIDDEN = 0, 1, 2, 4, 5
GATHERS = 7


def dot(a, b, contract=((1,), (0,))):
    return lax.dot_general(a, b, (contract, ((), ())), preferred_element_type=F32)


def two_part(values):
    high = values.astype(BF16)
    return high, (values - high.astype(F32)).astype(BF16)


def rms(total, count):
    return lax.rsqrt(total * (1.0 / count) + 1e-06)


def silu(v):
    return v / (1.0 + jnp.exp(-v))


def layer_kernel(
    n_seq, n_head,
    tok, wq, wk, wv, wo, sg, su, sd, eg, eu, ed, ids_row,
    out,
    x, own, wqkv, wo_v, sd_v, ed_v, sgu, egu, qkv, st, got, pre, car, att,
    hn, mid, rin, outb, hs, hr, rout, back, res, chosen, chosen_t, acc, sq,
    load_sem, w_send, w_recv, s_send, s_recv, g_send, g_recv,
):
    rows, width = x.shape
    cols = width // n_head
    owned = eg.shape[0]
    hidden = eg.shape[2]
    span = 2 * HD
    per = n_seq // 2
    s = lax.axis_index("seq")
    h = lax.axis_index("head")
    core = h % 2
    chip = h // 2
    chips = n_head // 2
    deep = n_seq // NY
    lay = s // deep
    partner = 2 * chip + 1 - core
    right = 2 * ((chip + 1) % chips) + core
    left = 2 * ((chip + chips - 1) % chips) + core
    far = 2 * ((chip + 2) % chips) + core

    def twin(b):
        return 2 * (b // 2) + 1 - b % 2

    def col_slice(index, size):
        return pl.ds(pl.multiple_of(index * size, 128), size)

    def load(i, src, dst):
        return pltpu.make_async_copy(src, dst, load_sem.at[i])

    loads = [
        load(0, tok, x),
        load(1, wq, wqkv.at[:, pl.ds(0, span)]),
        load(2, wk, wqkv.at[:, pl.ds(span, span)]),
        load(3, wv, wqkv.at[:, pl.ds(2 * span, span)]),
        load(4, tok.at[:, col_slice(h, cols)], own),
        load(5, wo.at[:, col_slice(h, cols)], wo_v.at[h]),
        load(6, sd.at[:, col_slice(h, cols)], sd_v.at[h]),
        load(7, ed.at[:, :, col_slice(h, cols)], ed_v.at[h]),
        load(8, sg, sgu.at[:, pl.ds(0, hidden)]),
        load(9, su, sgu.at[:, pl.ds(hidden, hidden)]),
        load(10, eg, egu.at[:, :, pl.ds(0, hidden)]),
        load(11, eu, egu.at[:, :, pl.ds(hidden, hidden)]),
    ]

    def seq_peer(t):
        return (s + t) % n_seq

    def head_peer(t):
        return (h + t) % n_head

    barrier = pltpu.get_barrier_semaphore()

    def greet_seq(t, carry):
        pl.semaphore_signal(barrier, inc=1, device_id={"seq": seq_peer(t)})
        return carry

    def greet_head(t, carry):
        pl.semaphore_signal(barrier, inc=1, device_id={"head": head_peer(t)})
        return carry

    for copy in loads[:4]:
        copy.start()
    lax.fori_loop(1, n_head, greet_head, 0)
    lax.fori_loop(1, n_seq, greet_seq, 0)
    for copy in loads[4:]:
        copy.start()

    def part_of(i):
        n = (wo_v, sd_v)[i].shape[1] // NY
        return pl.ds(pl.multiple_of(lay * n, n), n)

    def weight_copy(i, peer):
        at = col_slice(peer, cols)
        if i == 2:
            src, dst = ed.at[:, :, at], ed_v.at[h]
        else:
            src, dst = (wo, sd)[i].at[part_of(i), at], (wo_v, sd_v)[i].at[h, part_of(i)]
        return pltpu.make_async_remote_copy(
            src, dst, w_send.at[i], w_recv.at[i], device_id={"head": peer}
        )

    def weight_bytes(i):
        some = pl.ds(0, n_head - 1)
        if i == 2:
            ref = ed_v.at[some]
        elif i < 2:
            ref = (wo_v, sd_v)[i].at[some, pl.ds(0, (wo_v, sd_v)[i].shape[1] // NY)]
        else:
            whole = (wo_v, sd_v)[i - 3]
            ref = whole.at[some, pl.ds(0, whole.shape[1] // NY * (NY - 1))]
        return pltpu.make_async_remote_copy(
            ref, ref, w_send.at[i], w_recv.at[i], device_id={"head": partner}
        )

    def weight_share(i):
        whole = (wo_v, sd_v)[i]

        def one(t, carry):
            ref = whole.at[head_peer(t), part_of(i)]
            for k in (2, 1, 3):
                pltpu.make_async_remote_copy(
                    ref, ref, w_send.at[3 + i], w_recv.at[3 + i],
                    device_id={"seq": ((lay + k) % NY) * deep + s % deep},
                ).start()
            return carry

        lax.fori_loop(1, n_head, one, 0)

    def seq_refs(e):
        if e == STATE:
            return st, got
        if e == CARRY:
            return pre, car
        if e >= RETURN:
            return rout.at[e - RETURN], back.at[e - RETURN]
        return outb.at[e - DISPATCH], rin.at[h, e - DISPATCH]

    def seq_start(e):
        src, dst = seq_refs(e)

        def one(t, carry):
            peer = seq_peer(t)
            pltpu.make_async_remote_copy(
                src.at[peer], dst.at[s], s_send.at[e], s_recv.at[e], device_id={"seq": peer}
            ).start()
            return carry

        lax.fori_loop(1, n_seq, one, 0)

    def seq_bytes(e):
        src, dst = seq_refs(e)
        some = pl.ds(0, n_seq - 1)
        return pltpu.make_async_remote_copy(
            src.at[some], dst.at[some], s_send.at[e], s_recv.at[e],
            device_id={"seq": seq_peer(1)},
        )

    def view(g, b):
        if g == HEADS:
            return hn.at[b]
        if g == MIDDLE:
            return mid.at[b]
        if g == SHARED_HIDDEN:
            return hs.at[b]
        if g >= ROUTED_HIDDEN:
            return hr.at[b, g - ROUTED_HIDDEN]
        return rin.at[b, g - ROUTED]

    def half(g, b, k):
        whole = view(g, b)
        n = whole.shape[0] // 2
        return whole.at[pl.ds(k * n, n)]

    def leg(g, ref, i, target):
        return pltpu.make_async_remote_copy(
            ref, ref, g_send.at[g], g_recv.at[g, i], device_id={"head": target}
        )

    FROM_LEFT, FROM_RIGHT, FROM_TWIN, FAR, TWIN_LEFT, TWIN_RIGHT, TWIN_FAR = range(7)

    def arrived(g, i):
        b = (left, right, partner, far, twin(left), twin(right), twin(far))[i]
        leg(g, view(g, b), i, partner).wait_recv()
        return b

    def gather_start(g):
        leg(g, view(g, h), FROM_LEFT, right).start()
        leg(g, view(g, h), FROM_RIGHT, left).start()
        leg(g, view(g, h), FROM_TWIN, partner).start()

    def gather_pass(g):
        arrived(g, FROM_LEFT)
        leg(g, half(g, left, 0), FAR, right).start()
        leg(g, view(g, left), TWIN_LEFT, partner).start()
        arrived(g, FROM_RIGHT)
        leg(g, half(g, right, 1), FAR, left).start()
        leg(g, view(g, right), TWIN_RIGHT, partner).start()

    def gather_far(g):
        arrived(g, FAR)
        leg(g, view(g, far), TWIN_FAR, partner).start()

    def gather_sent(g):
        some = pl.ds(0, n_head - 1)
        ref = view(g, some)
        leg(g, ref, 0, partner).wait_send()

    for i in (0, 1, 2, 3):
        loads[i].wait()
    block = min(256, rows)

    def square_sum(ref, at, count):
        total = None
        for j in range(count // 128):
            wide = ref[at, j * 128 : (j + 1) * 128].astype(F32)
            total = wide * wide if total is None else total + wide * wide
        return total

    def project(i, carry):
        at = pl.ds(pl.multiple_of(i * block, block), block)
        scale = rms(jnp.sum(square_sum(x, at, width), axis=-1, keepdims=True), width)
        qkv[at, :] = (dot(x[at, :], wqkv[...]) * scale).astype(BF16)
        return carry

    lax.fori_loop(0, rows // block, project, 0)

    for a in range(2):
        k = qkv[:, span + a * HD : span + (a + 1) * HD]
        v = qkv[:, 2 * span + a * HD : 2 * span + (a + 1) * HD]
        st[a * per : (a + 1) * per] = dot(k, v, ((0,), (0,))).reshape(per, -1, HD)

    for a in range(2):
        for i in range(rows // block):
            top, end = i * block, (i + 1) * block
            q = qkv[top:end, a * HD : (a + 1) * HD]
            k = qkv[:end, span + a * HD : span + (a + 1) * HD]
            v = qkv[:end, 2 * span + a * HD : 2 * span + (a + 1) * HD]
            scores = dot(q, k, ((1,), (1,)))
            row = lax.broadcasted_iota(jnp.int32, scores.shape, 0) + top
            col = lax.broadcasted_iota(jnp.int32, scores.shape, 1)
            high, low = two_part(jnp.where(row >= col, scores, 0.0))
            att[top:end, a * HD : (a + 1) * HD] = dot(high, v) + dot(low, v)

    ids_r = ids_row[...]
    ids_c = jnp.transpose(jnp.broadcast_to(ids_r.astype(F32), (128, rows)))[:, :1].astype(jnp.int32)
    row = lax.broadcasted_iota(jnp.int32, (rows, rows), 0)
    col = lax.broadcasted_iota(jnp.int32, (rows, rows), 1)
    same = ids_c == ids_r
    rank_r = jnp.sum(jnp.where(same & (row <= col), 1.0, 0.0), axis=0, keepdims=True)
    rank_c = jnp.sum(jnp.where(same & (col <= row), 1.0, 0.0), axis=1, keepdims=True)
    taken = n_seq * CAP
    slots = owned * taken

    def base(ids, rank):
        place = (ids & 1) * taken + (ids >> 1) * CAP
        return place.astype(F32) + (rank - 1.0)

    place = lax.broadcasted_iota(jnp.int32, (slots, 1), 0).astype(F32)
    chosen[...] = jnp.where(place == base(ids_r, rank_r), 1.0, 0.0).astype(BF16)
    place = lax.broadcasted_iota(jnp.int32, (1, slots), 1).astype(F32)
    chosen_t[...] = jnp.where(place == base(ids_c, rank_c), 1.0, 0.0).astype(BF16)

    pl.semaphore_wait(barrier, n_head - 1 + n_seq - 1)
    for i in range(3):

        def one(t, carry):
            weight_copy(i, head_peer(t)).start()
            return carry

        lax.fori_loop(1, n_head, one, 0)
    seq_start(STATE)
    got[s] = st[s]
    seq_bytes(STATE).wait_recv()

    def running(j, total):
        pre[j] = total
        return total + got[j]

    lax.fori_loop(0, n_seq, running, jnp.zeros(pre.shape[1:], F32))
    seq_start(CARRY)
    car[s] = pre[s]
    weight_bytes(0).wait_recv()
    weight_share(0)

    seq_bytes(CARRY).wait_recv()
    for a in range(2):
        high, low = two_part(car[a * per : (a + 1) * per].reshape(HD, HD))
        q = qkv[:, a * HD : (a + 1) * HD]
        whole = att[:, a * HD : (a + 1) * HD] + dot(q, high) + dot(q, low)
        scale = rms(jnp.sum(whole * whole, axis=-1, keepdims=True), HD)
        hn[h, :, a * HD : (a + 1) * HD] = (whole * scale).astype(BF16)
    gather_start(HEADS)

    loads[4].wait()
    res[...] = own[...].astype(F32)
    loads[5].wait()
    weight_bytes(3).wait_recv()

    def use_heads(b):
        res[...] += dot(hn[b], wo_v[b])

    use_heads(h)
    use_heads(arrived(HEADS, FROM_TWIN))
    gather_pass(HEADS)
    use_heads(left)
    use_heads(right)
    gather_far(HEADS)
    use_heads(far)
    for i in (TWIN_LEFT, TWIN_RIGHT, TWIN_FAR):
        use_heads(arrived(HEADS, i))
    mid[h] = res[...].astype(BF16)
    gather_start(MIDDLE)
    for e in range(owned):
        picked = dot(chosen[e * taken : (e + 1) * taken, :], mid[h])
        outb[e] = picked.astype(BF16).reshape(outb.shape[1:])
        seq_start(DISPATCH + e)
        rin[h, e, s] = outb[e, s]
    weight_bytes(1).wait_recv()
    weight_share(1)

    loads[8].wait()
    loads[9].wait()
    acc[...] = jnp.zeros_like(acc)
    sq[...] = jnp.zeros_like(sq)

    def columns_of(b):
        return pl.ds(pl.multiple_of(b * cols, cols), cols)

    def add_squares(slot, part):
        wide = part.astype(F32)
        wide = wide * wide
        total = wide[:, :128]
        for j in range(1, cols // 128):
            total += wide[:, j * 128 : (j + 1) * 128]
        sq[slot, pl.ds(0, part.shape[0]), :] += total

    def use_middle(b):
        part = mid[b]
        acc[0, pl.ds(0, rows), :] += dot(part, sgu[columns_of(b), :])
        add_squares(0, part)

    def use_routed(e, b):
        part = rin[b, e].reshape(taken, cols)
        acc[1 + e, pl.ds(0, taken), :] += dot(part, egu[e, columns_of(b), :])
        add_squares(1 + e, part)

    def activate(slot, count):
        at = pl.ds(0, count)
        scale = rms(jnp.sum(sq[slot, at, :], axis=-1, keepdims=True), width)
        gate = acc[slot, at, pl.ds(0, hidden)] * scale
        up = acc[slot, at, pl.ds(hidden, hidden)] * scale
        return (silu(gate) * up).astype(BF16)

    use_middle(h)
    use_middle(arrived(MIDDLE, FROM_TWIN))
    gather_pass(MIDDLE)
    use_middle(left)
    use_middle(right)
    seq_bytes(DISPATCH).wait_recv()
    gather_start(ROUTED)
    gather_far(MIDDLE)
    use_middle(far)
    for i in (TWIN_LEFT, TWIN_RIGHT, TWIN_FAR):
        use_middle(arrived(MIDDLE, i))
    hs[h] = activate(0, rows)
    gather_start(SHARED_HIDDEN)

    loads[10].wait()
    loads[11].wait()
    use_routed(0, h)
    gather_pass(ROUTED)
    seq_bytes(DISPATCH + 1).wait_recv()
    gather_start(ROUTED + 1)
    use_routed(0, arrived(ROUTED, FROM_TWIN))
    use_routed(0, left)
    use_routed(0, right)
    gather_pass(SHARED_HIDDEN)
    gather_far(ROUTED)
    use_routed(0, far)
    for i in (TWIN_LEFT, TWIN_RIGHT, TWIN_FAR):
        use_routed(0, arrived(ROUTED, i))
    hr[h, 0] = activate(1, taken)
    gather_pass(ROUTED + 1)
    gather_start(ROUTED_HIDDEN)
    use_routed(1, h)
    use_routed(1, arrived(ROUTED + 1, FROM_TWIN))
    use_routed(1, left)
    use_routed(1, right)
    gather_far(SHARED_HIDDEN)
    gather_far(ROUTED + 1)
    use_routed(1, far)
    for i in (TWIN_LEFT, TWIN_RIGHT, TWIN_FAR):
        use_routed(1, arrived(ROUTED + 1, i))
    hr[h, 1] = activate(2, taken)
    gather_start(ROUTED_HIDDEN + 1)

    loads[6].wait()
    loads[7].wait()
    weight_bytes(2).wait_recv()

    def use_shared(b):
        res[...] += dot(hs[b], sd_v[b])

    def use_hidden(e, b):
        acc[1 + e, pl.ds(0, taken), pl.ds(0, cols)] += dot(hr[b, e], ed_v[b, e])

    for e in range(owned):
        acc[1 + e] = jnp.zeros(acc.shape[1:], F32)
    gather_pass(ROUTED_HIDDEN)
    use_hidden(0, h)
    use_hidden(0, arrived(ROUTED_HIDDEN, FROM_TWIN))
    use_hidden(0, left)
    use_hidden(0, right)
    gather_far(ROUTED_HIDDEN)
    gather_pass(ROUTED_HIDDEN + 1)
    use_hidden(0, far)
    for i in (TWIN_LEFT, TWIN_RIGHT, TWIN_FAR):
        use_hidden(0, arrived(ROUTED_HIDDEN, i))

    def give_back(e):
        result = acc[1 + e, pl.ds(0, taken), pl.ds(0, cols)]
        rout[e] = result.astype(BF16).reshape(rout.shape[1:])
        seq_start(RETURN + e)
        back[e, s] = rout[e, s]

    give_back(0)
    use_hidden(1, h)
    use_hidden(1, arrived(ROUTED_HIDDEN + 1, FROM_TWIN))
    use_hidden(1, left)
    use_hidden(1, right)
    gather_far(ROUTED_HIDDEN + 1)
    use_hidden(1, far)
    for i in (TWIN_LEFT, TWIN_RIGHT, TWIN_FAR):
        use_hidden(1, arrived(ROUTED_HIDDEN + 1, i))
    give_back(1)

    weight_bytes(4).wait_recv()
    for b in (h, left, right, far):
        use_shared(b)
    for i in (FROM_TWIN, TWIN_LEFT, TWIN_RIGHT, TWIN_FAR):
        use_shared(arrived(SHARED_HIDDEN, i))
    seq_bytes(RETURN).wait_recv()
    res[...] += dot(chosen_t[:, :taken], back[0].reshape(taken, cols))
    seq_bytes(RETURN + 1).wait_recv()
    routed = dot(chosen_t[:, taken:], back[1].reshape(taken, cols))
    out[...] = (res[...] + routed).astype(BF16)

    for i in range(5):
        weight_bytes(i).wait_send()
    for e in range(EXCHANGES):
        seq_bytes(e).wait_send()
    for g in range(GATHERS):
        gather_sent(g)


def shards(
    tokens,
    w_query,
    w_key,
    w_value,
    w_out,
    shared_gate,
    shared_up,
    shared_down,
    expert_gate,
    expert_up,
    expert_down,
    expert_ids,
):
    n_seq, n_head = lax.axis_size("seq"), lax.axis_size("head")
    rows, width = tokens.shape
    cols = width // n_head
    owned, _, hidden = expert_gate.shape
    heads = w_query.shape[1]
    taken = n_seq * CAP
    slots = owned * taken
    chunk = heads // n_seq
    most = max(rows, taken)
    any_spec = pl.BlockSpec(memory_space=pl.ANY)
    vmem_spec = pl.BlockSpec(memory_space=pltpu.VMEM)
    V = pltpu.VMEM
    dma = pltpu.SemaphoreType.DMA
    return pl.pallas_call(
        functools.partial(layer_kernel, n_seq, n_head),
        out_shape=jax.ShapeDtypeStruct((rows, cols), BF16),
        in_specs=[any_spec] * 11 + [vmem_spec],
        out_specs=vmem_spec,
        scratch_shapes=[
            V((rows, width), BF16),
            V((rows, cols), BF16),
            V((width, 3 * heads), BF16),
            V((n_head, heads, cols), BF16),
            V((n_head, hidden, cols), BF16),
            V((n_head, owned, hidden, cols), BF16),
            V((width, 2 * hidden), BF16),
            V((owned, width, 2 * hidden), BF16),
            V((rows, 3 * heads), BF16),
            V((n_seq, chunk, HD), F32),
            V((n_seq, chunk, HD), F32),
            V((n_seq, chunk, HD), F32),
            V((n_seq, chunk, HD), F32),
            V((rows, heads), F32),
            V((n_head, rows, heads), BF16),
            V((n_head, rows, cols), BF16),
            V((n_head, owned, n_seq, CAP, cols), BF16),
            V((owned, n_seq, CAP, cols), BF16),
            V((n_head, rows, hidden), BF16),
            V((n_head, owned, taken, hidden), BF16),
            V((owned, n_seq, CAP, cols), BF16),
            V((owned, n_seq, CAP, cols), BF16),
            V((rows, cols), F32),
            V((slots, rows), BF16),
            V((rows, slots), BF16),
            V((1 + owned, most, 2 * hidden), F32),
            V((1 + owned, most, HD), F32),
            dma((12,)),
            dma((5,)),
            dma((5,)),
            dma((EXCHANGES,)),
            dma((EXCHANGES,)),
            dma((GATHERS,)),
            dma((GATHERS, 7)),
        ],
        compiler_params=pltpu.CompilerParams(
            collective_id=0, has_side_effects=True, vmem_limit_bytes=60 * 1024 * 1024
        ),
    )(
        tokens, w_query, w_key, w_value, w_out, shared_gate, shared_up, shared_down,
        expert_gate, expert_up, expert_down, expert_ids.reshape(1, rows),
    )


def solution(mesh):
    return jax.shard_map(
        shards,
        mesh=mesh,
        in_specs=(
            P("seq", None),
            P(None, "head"),
            P(None, "head"),
            P(None, "head"),
            P("head", None),
            P(None, "head"),
            P(None, "head"),
            P("head", None),
            P("seq", None, "head"),
            P("seq", None, "head"),
            P("seq", "head", None),
            P("seq", None),
        ),
        out_specs=P("seq", "head"),
        check_vma=False,
    )
```

```python
import functools

import jax
import jax.numpy as jnp
from jax import lax
from jax.experimental import pallas as pl
from jax.experimental.pallas import tpu as pltpu
from jax.sharding import PartitionSpec as P

HD = 128
CAP = 16
NY = 4
AHEAD = 4
LOTS = ((0, 0), (0, 1), (1, 0), (1, 1))
F32 = jnp.float32
BF16 = jnp.bfloat16

STATE, CARRY, DISPATCH, RETURN = 0, 1, 2, 6
EXCHANGES = 8
HEADS, MIDDLE, SHARED_HIDDEN, ROUTED, ROUTED_HIDDEN = 0, 2, 4, 5, 9
GATHERS = 13


def dot(a, b, contract=((1,), (0,))):
    return lax.dot_general(a, b, (contract, ((), ())), preferred_element_type=F32)


def two_part(values):
    high = values.astype(BF16)
    return high, (values - high.astype(F32)).astype(BF16)


def rms(total, count):
    return lax.rsqrt(total * (1.0 / count) + 1e-06)


def silu(v):
    return v / (1.0 + jnp.exp(-v))


def layer_kernel(
    n_seq, n_head,
    tok, wq, wk, wv, wo, sg, su, sd, eg, eu, ed, ids_row,
    out,
    x, own, wqkv, wo_v, sd_v, ed_v, sgu, egu, qkv, st, got, pre, car, att,
    hn, mid, rin, outb, hs, hr, rout, back, res, chosen, chosen_t, acc, sq,
    load_sem, w_send, w_recv, s_send, s_recv, g_send, g_recv,
):
    rows, width = x.shape
    cols = width // n_head
    owned = eg.shape[0]
    hidden = eg.shape[2]
    span = 2 * HD
    per = n_seq // 2
    s = lax.axis_index("seq")
    h = lax.axis_index("head")
    core = h % 2
    chip = h // 2
    chips = n_head // 2
    deep = n_seq // NY
    lay = s // deep
    partner = 2 * chip + 1 - core
    right = 2 * ((chip + 1) % chips) + core
    left = 2 * ((chip + chips - 1) % chips) + core
    far = 2 * ((chip + 2) % chips) + core

    def twin(b):
        return 2 * (b // 2) + 1 - b % 2

    def col_slice(index, size):
        return pl.ds(pl.multiple_of(index * size, 128), size)

    def load(i, src, dst):
        return pltpu.make_async_copy(src, dst, load_sem.at[i])

    loads = [
        load(0, tok, x),
        load(1, wq, wqkv.at[:, pl.ds(0, span)]),
        load(2, wk, wqkv.at[:, pl.ds(span, span)]),
        load(3, wv, wqkv.at[:, pl.ds(2 * span, span)]),
        load(4, tok.at[:, col_slice(h, cols)], own),
        load(5, wo.at[:, col_slice(h, cols)], wo_v.at[h]),
        load(6, sd.at[:, col_slice(h, cols)], sd_v.at[h]),
        load(7, ed.at[:, :, col_slice(h, cols)], ed_v.at[h]),
        load(8, sg, sgu.at[:, pl.ds(0, hidden)]),
        load(9, su, sgu.at[:, pl.ds(hidden, hidden)]),
        load(10, eg, egu.at[:, :, pl.ds(0, hidden)]),
        load(11, eu, egu.at[:, :, pl.ds(hidden, hidden)]),
    ]

    def seq_peer(t):
        return (s + t) % n_seq

    def head_peer(t):
        return (h + t) % n_head

    barrier = pltpu.get_barrier_semaphore()

    def greet_seq(t, carry):
        pl.semaphore_signal(barrier, inc=1, device_id={"seq": seq_peer(t)})
        return carry

    def greet_head(t, carry):
        pl.semaphore_signal(barrier, inc=1, device_id={"head": head_peer(t)})
        return carry

    for copy in loads[:4]:
        copy.start()
    lax.fori_loop(1, n_head, greet_head, 0)
    lax.fori_loop(1, n_seq, greet_seq, 0)
    for copy in loads[4:]:
        copy.start()

    def part_of(i):
        n = (wo_v, sd_v)[i].shape[1] // NY
        return pl.ds(pl.multiple_of(lay * n, n), n)

    def weight_copy(i, peer):
        at = col_slice(peer, cols)
        if i >= 5:
            e, part = LOTS[i - 5]
            part = pl.ds(part * (hidden // 2), hidden // 2)
            src, dst = ed.at[e, part, at], ed_v.at[h, e, part]
        else:
            src, dst = (wo, sd)[i].at[part_of(i), at], (wo_v, sd_v)[i].at[h, part_of(i)]
        return pltpu.make_async_remote_copy(
            src, dst, w_send.at[i], w_recv.at[i], device_id={"head": peer}
        )

    def weight_bytes(i):
        some = pl.ds(0, n_head - 1)
        if i >= 5:
            ref = ed_v.at[some, 0, pl.ds(0, hidden // 2)]
        elif i < 2:
            ref = (wo_v, sd_v)[i].at[some, pl.ds(0, (wo_v, sd_v)[i].shape[1] // NY)]
        else:
            whole = (wo_v, sd_v)[i - 3]
            ref = whole.at[some, pl.ds(0, whole.shape[1] // NY * (NY - 1))]
        return pltpu.make_async_remote_copy(
            ref, ref, w_send.at[i], w_recv.at[i], device_id={"head": partner}
        )

    def weight_share(i, first=1, end=None):
        whole = (wo_v, sd_v)[i]

        def one(t, carry):
            ref = whole.at[head_peer(t), part_of(i)]
            for k in (2, 1, 3):
                pltpu.make_async_remote_copy(
                    ref, ref, w_send.at[3 + i], w_recv.at[3 + i],
                    device_id={"seq": ((lay + k) % NY) * deep + s % deep},
                ).start()
            return carry

        lax.fori_loop(first, end or n_head, one, 0)

    def seq_refs(e, peer):
        if e == STATE:
            return st.at[peer], got.at[s]
        if e == CARRY:
            return pre.at[peer], car.at[s]
        if e >= RETURN:
            return rout.at[e - RETURN, peer % 2, peer // 2], back.at[e - RETURN, s]
        e = (e - DISPATCH) // 2
        return outb.at[e, peer], rin.at[h, e, s % 2, s // 2]

    def seq_send(e, first, last, stride):
        def one(t, carry):
            peer = seq_peer(t * stride + first)
            src, dst = seq_refs(e, peer)
            pltpu.make_async_remote_copy(
                src, dst, s_send.at[e], s_recv.at[e], device_id={"seq": peer}
            ).start()
            return carry

        lax.fori_loop(0, last, one, 0)

    def seq_start(e):
        seq_send(e, 1, n_seq - 1, 1)

    def seq_bytes(e):
        ref = st if e == STATE else pre if e == CARRY else back.at[0]
        count = n_seq - 1
        if DISPATCH <= e < RETURN:
            count = n_seq // 2 - 1 + e % 2
        ref = ref.at[pl.ds(0, count)]
        return pltpu.make_async_remote_copy(
            ref, ref, s_send.at[e], s_recv.at[e], device_id={"seq": seq_peer(1)}
        )

    parity = s % 2
    middle = rows // 2

    def lot(c):
        return c // 2, (parity + c) % 2

    def view(g, b):
        if g < SHARED_HIDDEN:
            ref = hn if g < MIDDLE else mid
            return ref.at[b, pl.ds(g % 2 * middle, middle)]
        if g == SHARED_HIDDEN:
            return hs.at[b]
        e, side = lot((g - ROUTED) % 4)
        return (rin if g < ROUTED_HIDDEN else hr).at[b, e, side]

    def half(g, b, k):
        whole = view(g, b)
        n = whole.shape[0] // 2
        return whole.at[pl.ds(k * n, n)]

    def leg(g, ref, i, target):
        return pltpu.make_async_remote_copy(
            ref, ref, g_send.at[g], g_recv.at[g, i], device_id={"head": target}
        )

    FROM_LEFT, FROM_RIGHT, FROM_TWIN, FAR, TWIN_LEFT, TWIN_RIGHT, TWIN_FAR = range(7)

    def arrived(g, i):
        b = (left, right, partner, far, twin(left), twin(right), twin(far))[i]
        leg(g, view(g, b), i, partner).wait_recv()
        return b

    def gather_start(g):
        leg(g, view(g, h), FROM_LEFT, right).start()
        leg(g, view(g, h), FROM_RIGHT, left).start()
        leg(g, view(g, h), FROM_TWIN, partner).start()

    def gather_pass(g):
        arrived(g, FROM_LEFT)
        leg(g, half(g, left, 0), FAR, right).start()
        leg(g, view(g, left), TWIN_LEFT, partner).start()
        arrived(g, FROM_RIGHT)
        leg(g, half(g, right, 1), FAR, left).start()
        leg(g, view(g, right), TWIN_RIGHT, partner).start()

    def gather_far(g):
        arrived(g, FAR)
        leg(g, view(g, far), TWIN_FAR, partner).start()

    def gather_sent(g):
        some = pl.ds(0, n_head - 1)
        ref = view(g, some)
        leg(g, ref, 0, partner).wait_send()

    for i in (0, 1, 2, 3):
        loads[i].wait()
    block = min(256, rows)

    def square_sum(ref, at, count):
        total = None
        for j in range(count // 128):
            wide = ref[at, j * 128 : (j + 1) * 128].astype(F32)
            total = wide * wide if total is None else total + wide * wide
        return total

    def project(i, carry):
        at = pl.ds(pl.multiple_of(i * block, block), block)
        scale = rms(jnp.sum(square_sum(x, at, width), axis=-1, keepdims=True), width)
        qkv[at, :] = (dot(x[at, :], wqkv[...]) * scale).astype(BF16)
        return carry

    lax.fori_loop(0, rows // block, project, 0)

    for a in range(2):
        k = qkv[:, span + a * HD : span + (a + 1) * HD]
        v = qkv[:, 2 * span + a * HD : 2 * span + (a + 1) * HD]
        st[a * per : (a + 1) * per] = dot(k, v, ((0,), (0,))).reshape(per, -1, HD)

    for a in range(2):
        for i in range(rows // block):
            top, end = i * block, (i + 1) * block
            q = qkv[top:end, a * HD : (a + 1) * HD]
            k = qkv[:end, span + a * HD : span + (a + 1) * HD]
            v = qkv[:end, 2 * span + a * HD : 2 * span + (a + 1) * HD]
            scores = dot(q, k, ((1,), (1,)))
            row = lax.broadcasted_iota(jnp.int32, scores.shape, 0) + top
            col = lax.broadcasted_iota(jnp.int32, scores.shape, 1)
            high, low = two_part(jnp.where(row >= col, scores, 0.0))
            att[top:end, a * HD : (a + 1) * HD] = dot(high, v) + dot(low, v)

    ids_r = ids_row[...]
    ids_c = jnp.transpose(jnp.broadcast_to(ids_r.astype(F32), (128, rows)))[:, :1].astype(jnp.int32)
    row = lax.broadcasted_iota(jnp.int32, (rows, rows), 0)
    col = lax.broadcasted_iota(jnp.int32, (rows, rows), 1)
    same = ids_c == ids_r
    rank_r = jnp.sum(jnp.where(same & (row <= col), 1.0, 0.0), axis=0, keepdims=True)
    rank_c = jnp.sum(jnp.where(same & (col <= row), 1.0, 0.0), axis=1, keepdims=True)
    taken = n_seq * CAP
    slots = owned * taken

    def base(ids, rank):
        place = (ids & 1) * taken + (ids >> 1) * CAP
        return place.astype(F32) + (rank - 1.0)

    place = lax.broadcasted_iota(jnp.int32, (slots, 1), 0).astype(F32)
    chosen[...] = jnp.where(place == base(ids_r, rank_r), 1.0, 0.0).astype(BF16)
    place = lax.broadcasted_iota(jnp.int32, (1, slots), 1).astype(F32)
    chosen_t[...] = jnp.where(place == base(ids_c, rank_c), 1.0, 0.0).astype(BF16)

    pl.semaphore_wait(barrier, n_head - 1 + n_seq - 1)
    seq_start(STATE)
    got[s] = st[s]
    def weight_start(i):
        def one(t, carry):
            weight_copy(i, head_peer(t)).start()
            return carry

        lax.fori_loop(1, n_head, one, 0)

    weight_start(0)
    weight_start(1)
    for i in range(5, 5 + AHEAD):
        weight_start(i)
    seq_bytes(STATE).wait_recv()

    def running(j, total):
        pre[j] = total
        return total + got[j]

    lax.fori_loop(0, n_seq, running, jnp.zeros(pre.shape[1:], F32))
    seq_start(CARRY)
    car[s] = pre[s]
    weight_bytes(0).wait_recv()
    weight_share(0)

    seq_bytes(CARRY).wait_recv()
    for a in range(2):
        high, low = two_part(car[a * per : (a + 1) * per].reshape(HD, HD))
        q = qkv[:, a * HD : (a + 1) * HD]
        whole = att[:, a * HD : (a + 1) * HD] + dot(q, high) + dot(q, low)
        scale = rms(jnp.sum(whole * whole, axis=-1, keepdims=True), HD)
        hn[h, :, a * HD : (a + 1) * HD] = (whole * scale).astype(BF16)
    gather_start(HEADS)
    gather_start(HEADS + 1)

    loads[4].wait()
    res[...] = own[...].astype(F32)
    for k in range(2):
        gather_pass(HEADS + k)
    loads[5].wait()
    weight_bytes(3).wait_recv()

    def use_heads(k, b):
        at = pl.ds(k * middle, middle)
        res[at, :] += dot(hn[b, at, :], wo_v[b])

    for k in range(2):
        use_heads(k, h)
        use_heads(k, arrived(HEADS + k, FROM_TWIN))
        use_heads(k, left)
        use_heads(k, right)
    for k in range(2):
        gather_far(HEADS + k)
        use_heads(k, far)
        for i in (TWIN_LEFT, TWIN_RIGHT, TWIN_FAR):
            use_heads(k, arrived(HEADS + k, i))
        at = pl.ds(k * middle, middle)
        mid[h, at, :] = res[at, :].astype(BF16)
        gather_start(MIDDLE + k)
        if k == 0:
            for e in range(owned):
                own_lot = pl.ds(e * taken, taken)
                acc[1 + e, pl.ds(0, taken), pl.ds(0, cols)] = dot(chosen[own_lot, at], mid[h, at, :])
    for e in range(owned):
        at = pl.ds(middle, middle)
        picked = acc[1 + e, pl.ds(0, taken), pl.ds(0, cols)] + dot(
            chosen[pl.ds(e * taken, taken), at], mid[h, at, :]
        )
        outb[e] = picked.astype(BF16).reshape(outb.shape[1:])
        seq_send(DISPATCH + 2 * e, 2, n_seq // 2 - 1, 2)
        seq_send(DISPATCH + 2 * e + 1, 1, n_seq // 2, 2)
        rin[h, e, s % 2, s // 2] = outb[e, s]
    weight_bytes(1).wait_recv()
    weight_share(1)

    loads[8].wait()
    loads[9].wait()
    acc[...] = jnp.zeros_like(acc)
    sq[...] = jnp.zeros_like(sq)

    def columns_of(b):
        return pl.ds(pl.multiple_of(b * cols, cols), cols)

    def add_squares(slot, top, part):
        wide = part.astype(F32)
        wide = wide * wide
        total = wide[:, :128]
        for j in range(1, cols // 128):
            total += wide[:, j * 128 : (j + 1) * 128]
        sq[slot, pl.ds(top, part.shape[0]), :] += total

    def use_middle(k, b):
        at = pl.ds(k * middle, middle)
        part = mid[b, at, :]
        acc[0, at, :] += dot(part, sgu[columns_of(b), :])
        add_squares(0, k * middle, part)

    lot_rows = taken // 2

    def use_routed(c, b):
        e, side = lot(c)
        part = rin[b, e, side].reshape(lot_rows, cols)
        acc[1 + e, pl.ds(c % 2 * lot_rows, lot_rows), :] += dot(part, egu[e, columns_of(b), :])
        add_squares(1 + e, c % 2 * lot_rows, part)

    def activate(slot, top, count):
        at = pl.ds(top, count)
        scale = rms(jnp.sum(sq[slot, at, :], axis=-1, keepdims=True), width)
        gate = acc[slot, at, pl.ds(0, hidden)] * scale
        up = acc[slot, at, pl.ds(hidden, hidden)] * scale
        return (silu(gate) * up).astype(BF16)

    near = (left, right)
    last = (TWIN_LEFT, TWIN_RIGHT, TWIN_FAR)

    def begin(g, use):
        use(h)
        use(arrived(g, FROM_TWIN))
        for b in near:
            use(b)

    def end(g, use):
        use(far)
        for i in last:
            use(arrived(g, i))

    def routed(c):
        return functools.partial(use_routed, c)

    def hidden_of(c):
        e, side = lot(c)
        hr[h, e, side] = activate(1 + e, c % 2 * lot_rows, lot_rows)
        gather_start(ROUTED_HIDDEN + c)

    def shared(k):
        return functools.partial(use_middle, k)

    gather_pass(MIDDLE)
    begin(MIDDLE, shared(0))
    gather_pass(MIDDLE + 1)
    for i in range(5 + AHEAD, 9):
        weight_start(i)
    seq_bytes(DISPATCH).wait_recv()
    gather_start(ROUTED)
    gather_far(MIDDLE)
    begin(MIDDLE + 1, shared(1))
    seq_bytes(DISPATCH + 1).wait_recv()
    gather_start(ROUTED + 1)
    end(MIDDLE, shared(0))
    gather_far(MIDDLE + 1)
    end(MIDDLE + 1, shared(1))
    hs[h] = activate(0, 0, rows)
    gather_pass(ROUTED)
    seq_bytes(DISPATCH + 2).wait_recv()
    gather_start(ROUTED + 2)
    loads[10].wait()
    loads[11].wait()
    begin(ROUTED, routed(0))
    gather_pass(ROUTED + 1)
    seq_bytes(DISPATCH + 3).wait_recv()
    gather_start(ROUTED + 3)
    gather_far(ROUTED)
    end(ROUTED, routed(0))
    hidden_of(0)
    begin(ROUTED + 1, routed(1))
    gather_pass(ROUTED + 2)
    gather_far(ROUTED + 1)
    end(ROUTED + 1, routed(1))
    hidden_of(1)
    gather_pass(ROUTED_HIDDEN)
    begin(ROUTED + 2, routed(2))
    gather_pass(ROUTED + 3)
    gather_far(ROUTED + 2)
    end(ROUTED + 2, routed(2))
    hidden_of(2)

    loads[6].wait()
    loads[7].wait()
    for i in range(5, 9):
        weight_bytes(i).wait_recv()

    def use_shared(b):
        res[...] += dot(hs[b], sd_v[b])

    def give_back(c):
        e, side = lot(c)
        total = None
        for b in (h, left, right, far, partner, twin(left), twin(right), twin(far)):
            part = dot(hr[b, e, side], ed_v[b, e])
            total = part if total is None else total + part
        rout[e, side] = total.astype(BF16).reshape(rout.shape[2:])
        if c % 2 == 0:
            seq_send(RETURN + e, 2, n_seq // 2 - 1, 2)
            back[e, s] = rout[e, side, s // 2]
        else:
            seq_send(RETURN + e, 1, n_seq // 2, 2)

    def hidden_end(c):
        for i in (FROM_TWIN,) + last:
            arrived(ROUTED_HIDDEN + c, i)

    gather_far(ROUTED_HIDDEN)
    gather_pass(ROUTED_HIDDEN + 1)
    hidden_end(0)
    give_back(0)
    begin(ROUTED + 3, routed(3))
    gather_far(ROUTED + 3)
    end(ROUTED + 3, routed(3))
    hidden_of(3)
    gather_far(ROUTED_HIDDEN + 1)
    gather_pass(ROUTED_HIDDEN + 2)
    hidden_end(1)
    give_back(1)
    gather_far(ROUTED_HIDDEN + 2)
    gather_pass(ROUTED_HIDDEN + 3)
    gather_start(SHARED_HIDDEN)
    hidden_end(2)
    give_back(2)
    gather_far(ROUTED_HIDDEN + 3)
    hidden_end(3)
    give_back(3)

    weight_bytes(4).wait_recv()
    gather_pass(SHARED_HIDDEN)
    gather_far(SHARED_HIDDEN)
    for b in (h, left, right, far):
        use_shared(b)
    for i in (FROM_TWIN, TWIN_LEFT, TWIN_RIGHT, TWIN_FAR):
        use_shared(arrived(SHARED_HIDDEN, i))
    seq_bytes(RETURN).wait_recv()
    res[...] += dot(chosen_t[:, :taken], back[0].reshape(taken, cols))
    seq_bytes(RETURN + 1).wait_recv()
    final = dot(chosen_t[:, taken:], back[1].reshape(taken, cols))
    out[...] = (res[...] + final).astype(BF16)

    for i in (0, 1, 3, 4, 5, 6, 7, 8):
        weight_bytes(i).wait_send()
    for e in range(EXCHANGES):
        seq_bytes(e).wait_send()
    for g in range(GATHERS):
        gather_sent(g)


def shards(
    tokens,
    w_query,
    w_key,
    w_value,
    w_out,
    shared_gate,
    shared_up,
    shared_down,
    expert_gate,
    expert_up,
    expert_down,
    expert_ids,
):
    n_seq, n_head = lax.axis_size("seq"), lax.axis_size("head")
    rows, width = tokens.shape
    cols = width // n_head
    owned, _, hidden = expert_gate.shape
    heads = w_query.shape[1]
    taken = n_seq * CAP
    slots = owned * taken
    chunk = heads // n_seq
    most = max(rows, taken)
    any_spec = pl.BlockSpec(memory_space=pl.ANY)
    vmem_spec = pl.BlockSpec(memory_space=pltpu.VMEM)
    V = pltpu.VMEM
    dma = pltpu.SemaphoreType.DMA
    return pl.pallas_call(
        functools.partial(layer_kernel, n_seq, n_head),
        out_shape=jax.ShapeDtypeStruct((rows, cols), BF16),
        in_specs=[any_spec] * 11 + [vmem_spec],
        out_specs=vmem_spec,
        scratch_shapes=[
            V((rows, width), BF16),
            V((rows, cols), BF16),
            V((width, 3 * heads), BF16),
            V((n_head, heads, cols), BF16),
            V((n_head, hidden, cols), BF16),
            V((n_head, owned, hidden, cols), BF16),
            V((width, 2 * hidden), BF16),
            V((owned, width, 2 * hidden), BF16),
            V((rows, 3 * heads), BF16),
            V((n_seq, chunk, HD), F32),
            V((n_seq, chunk, HD), F32),
            V((n_seq, chunk, HD), F32),
            V((n_seq, chunk, HD), F32),
            V((rows, heads), F32),
            V((n_head, rows, heads), BF16),
            V((n_head, rows, cols), BF16),
            V((n_head, owned, 2, n_seq // 2, CAP, cols), BF16),
            V((owned, n_seq, CAP, cols), BF16),
            V((n_head, rows, hidden), BF16),
            V((n_head, owned, 2, taken // 2, hidden), BF16),
            V((owned, 2, n_seq // 2, CAP, cols), BF16),
            V((owned, n_seq, CAP, cols), BF16),
            V((rows, cols), F32),
            V((slots, rows), BF16),
            V((rows, slots), BF16),
            V((1 + owned, most, 2 * hidden), F32),
            V((1 + owned, most, HD), F32),
            dma((12,)),
            dma((9,)),
            dma((9,)),
            dma((EXCHANGES,)),
            dma((EXCHANGES,)),
            dma((GATHERS,)),
            dma((GATHERS, 7)),
        ],
        compiler_params=pltpu.CompilerParams(
            collective_id=0, has_side_effects=True, vmem_limit_bytes=60 * 1024 * 1024
        ),
    )(
        tokens, w_query, w_key, w_value, w_out, shared_gate, shared_up, shared_down,
        expert_gate, expert_up, expert_down, expert_ids.reshape(1, rows),
    )


def solution(mesh):
    return jax.shard_map(
        shards,
        mesh=mesh,
        in_specs=(
            P("seq", None),
            P(None, "head"),
            P(None, "head"),
            P(None, "head"),
            P("head", None),
            P(None, "head"),
            P(None, "head"),
            P("head", None),
            P("seq", None, "head"),
            P("seq", None, "head"),
            P("seq", "head", None),
            P("seq", None),
        ),
        out_specs=P("seq", "head"),
        check_vma=False,
    )
```

```python
import functools

import jax
import jax.numpy as jnp
from jax import lax
from jax.experimental import pallas as pl
from jax.experimental.pallas import tpu as pltpu
from jax.sharding import PartitionSpec as P

HD = 128
CAP = 16
NY = 4
F32 = jnp.float32
BF16 = jnp.bfloat16

STATE, CARRY, DISPATCH, RETURN = 0, 1, 2, 6
EXCHANGES = 8
HEADS, MIDDLE, SHARED_HIDDEN, ROUTED, ROUTED_HIDDEN = 0, 2, 4, 5, 9
GATHERS = 13


def dot(a, b, contract=((1,), (0,))):
    return lax.dot_general(a, b, (contract, ((), ())), preferred_element_type=F32)


def two_part(values):
    high = values.astype(BF16)
    return high, (values - high.astype(F32)).astype(BF16)


def rms(total, count):
    return lax.rsqrt(total * (1.0 / count) + 1e-06)


def silu(v):
    return v / (1.0 + jnp.exp(-v))


def layer_kernel(
    n_seq, n_head,
    tok, wq, wk, wv, wo, sg, su, sd, eg, eu, ed, ids_row,
    out,
    x, own, wqkv, wo_v, sd_v, ed_v, sgu, egu, qkv, st, got, pre, car, att,
    hn, mid, rin, outb, hs, hr, rout, back, res, chosen, chosen_t, acc, sq,
    load_sem, w_send, w_recv, s_send, s_recv, g_send, g_recv,
):
    rows, width = x.shape
    cols = width // n_head
    owned = eg.shape[0]
    hidden = eg.shape[2]
    span = 2 * HD
    per = n_seq // 2
    s = lax.axis_index("seq")
    h = lax.axis_index("head")
    core = h % 2
    chip = h // 2
    chips = n_head // 2
    deep = n_seq // NY
    lay = s // deep
    partner = 2 * chip + 1 - core
    right = 2 * ((chip + 1) % chips) + core
    left = 2 * ((chip + chips - 1) % chips) + core
    far = 2 * ((chip + 2) % chips) + core

    def twin(b):
        return 2 * (b // 2) + 1 - b % 2

    def col_slice(index, size):
        return pl.ds(pl.multiple_of(index * size, 128), size)

    def load(i, src, dst):
        return pltpu.make_async_copy(src, dst, load_sem.at[i])

    loads = [
        load(0, tok, x),
        load(1, wq, wqkv.at[:, pl.ds(0, span)]),
        load(1, wk, wqkv.at[:, pl.ds(span, span)]),
        load(1, wv, wqkv.at[:, pl.ds(2 * span, span)]),
        load(2, tok.at[:, col_slice(h, cols)], own),
        load(3, wo.at[:, col_slice(h, cols)], wo_v.at[h]),
        load(4, sd.at[:, col_slice(h, cols)], sd_v.at[h]),
        load(5, ed.at[:, :, col_slice(h, cols)], ed_v.at[h]),
        load(6, sg, sgu.at[:, pl.ds(0, hidden)]),
        load(6, su, sgu.at[:, pl.ds(hidden, hidden)]),
        load(7, eg, egu.at[:, :, pl.ds(0, hidden)]),
        load(7, eu, egu.at[:, :, pl.ds(hidden, hidden)]),
    ]

    def loaded(i):
        ref = (x, wqkv, own, wo_v.at[h], sd_v.at[h], ed_v.at[h], sgu, egu)[i]
        load(i, ref, ref).wait()

    def seq_peer(t):
        return (s + t) % n_seq

    def head_peer(t):
        return (h + t) % n_head

    barrier = pltpu.get_barrier_semaphore()

    def greet_seq(t, carry):
        pl.semaphore_signal(barrier, inc=1, device_id={"seq": seq_peer(t)})
        return carry

    def greet_head(t, carry):
        pl.semaphore_signal(barrier, inc=1, device_id={"head": head_peer(t)})
        return carry

    for copy in loads[:4]:
        copy.start()
    lax.fori_loop(1, n_head, greet_head, 0)
    lax.fori_loop(1, n_seq, greet_seq, 0)
    for copy in loads[4:]:
        copy.start()

    def part_of(i):
        n = (wo_v, sd_v)[i].shape[1] // NY
        return pl.ds(pl.multiple_of(lay * n, n), n)

    def ed_lines(i):
        early = hidden // 4 * 3
        return pl.ds(0, early) if i == 2 else pl.ds(early, hidden - early)

    def weight_copy(i, peer):
        at = col_slice(peer, cols)
        if i in (2, 5):
            lines = ed_lines(i)
            src, dst = ed.at[:, lines, at], ed_v.at[h, :, lines]
        else:
            src, dst = (wo, sd)[i].at[part_of(i), at], (wo_v, sd_v)[i].at[h, part_of(i)]
        return pltpu.make_async_remote_copy(
            src, dst, w_send.at[i], w_recv.at[i], device_id={"head": peer}
        )

    def weight_bytes(i):
        some = pl.ds(0, n_head - 1)
        if i in (2, 5):
            ref = ed_v.at[some, :, ed_lines(i)]
        elif i < 2:
            ref = (wo_v, sd_v)[i].at[some, pl.ds(0, (wo_v, sd_v)[i].shape[1] // NY)]
        else:
            whole = (wo_v, sd_v)[i - 3]
            ref = whole.at[some, pl.ds(0, whole.shape[1] // NY * (NY - 1))]
        return pltpu.make_async_remote_copy(
            ref, ref, w_send.at[i], w_recv.at[i], device_id={"head": partner}
        )

    def weight_share(i, first=1, end=None):
        whole = (wo_v, sd_v)[i]

        def one(t, carry):
            ref = whole.at[head_peer(t), part_of(i)]
            for k in (2, 1, 3):
                pltpu.make_async_remote_copy(
                    ref, ref, w_send.at[3 + i], w_recv.at[3 + i],
                    device_id={"seq": ((lay + k) % NY) * deep + s % deep},
                ).start()
            return carry

        lax.fori_loop(first, end or n_head, one, 0)

    def seq_refs(e, peer):
        if e == STATE:
            return st.at[peer], got.at[s]
        if e == CARRY:
            return pre.at[peer], car.at[s]
        if e >= RETURN:
            return rout.at[e - RETURN, peer % 2, peer // 2], back.at[e - RETURN, s]
        e = (e - DISPATCH) // 2
        return outb.at[e, peer], rin.at[h, e, s % 2, s // 2]

    def source_of(e):
        return min(e, DISPATCH) + (e >= RETURN)

    def seq_send(e, first, last, stride):
        def one(t, carry):
            peer = seq_peer(t * stride + first)
            src, dst = seq_refs(e, peer)
            pltpu.make_async_remote_copy(
                src, dst, s_send.at[source_of(e)], s_recv.at[e], device_id={"seq": peer}
            ).start()
            return carry

        lax.fori_loop(0, last, one, 0)

    def seq_start(e):
        seq_send(e, 1, n_seq - 1, 1)

    def seq_bytes(e):
        ref = st if e == STATE else pre if e == CARRY else back.at[0]
        count = n_seq - 1
        if DISPATCH <= e < RETURN:
            count = n_seq // 2 - 1 + e % 2
        ref = ref.at[pl.ds(0, count)]
        return pltpu.make_async_remote_copy(
            ref, ref, s_send.at[source_of(e)], s_recv.at[e], device_id={"seq": seq_peer(1)}
        )

    def seq_sent(e):
        some = pl.ds(0, n_seq - 1)
        ref = st if e == STATE else pre if e == CARRY else back
        ref = ref.at[some] if e < DISPATCH else ref.at[:, some]
        pltpu.make_async_remote_copy(
            ref, ref, s_send.at[source_of(e)], s_recv.at[e], device_id={"seq": seq_peer(1)}
        ).wait_send()

    parity = s % 2
    middle = rows // 2

    def lot(c):
        return c // 2, (parity + c) % 2

    def view(g, b):
        if g < SHARED_HIDDEN:
            ref = hn if g < MIDDLE else mid
            return ref.at[b, pl.ds(g % 2 * middle, middle)]
        if g == SHARED_HIDDEN:
            return hs.at[b]
        e, side = lot((g - ROUTED) % 4)
        return (rin if g < ROUTED_HIDDEN else hr).at[b, e, side]

    def half(g, b, k):
        whole = view(g, b)
        n = whole.shape[0] // 2
        return whole.at[pl.ds(k * n, n)]

    def buffer_of(g):
        return (g >= MIDDLE) + (g >= SHARED_HIDDEN) + (g >= ROUTED) + (g >= ROUTED_HIDDEN)

    def leg(g, ref, i, target):
        return pltpu.make_async_remote_copy(
            ref, ref, g_send.at[buffer_of(g)], g_recv.at[g, i], device_id={"head": target}
        )

    NEAR, FAR, TWIN = range(3)

    def arrived(g, i):
        count = (3, 1, 3)[i]
        leg(g, view(g, pl.ds(0, count)), i, partner).wait_recv()

    twins = (twin(left), twin(right), twin(far))

    def gather_start(g):
        for target in (right, left, partner):
            leg(g, view(g, h), NEAR, target).start()

    def gather_pass(g):
        arrived(g, NEAR)
        leg(g, half(g, left, 0), FAR, right).start()
        leg(g, half(g, right, 1), FAR, left).start()
        leg(g, view(g, left), TWIN, partner).start()
        leg(g, view(g, right), TWIN, partner).start()

    def gather_far(g):
        arrived(g, FAR)
        leg(g, view(g, far), TWIN, partner).start()

    def gather_sent(g):
        ref = (hn, mid, hs, rin, hr)[buffer_of(g)].at[pl.ds(0, n_head - 1)]
        leg(g, ref, 0, partner).wait_send()

    loaded(0)
    loaded(1)
    block = min(256, rows)

    def square_sum(ref, at, count):
        total = None
        for j in range(count // 128):
            wide = ref[at, j * 128 : (j + 1) * 128].astype(F32)
            total = wide * wide if total is None else total + wide * wide
        return total

    def project(i, carry):
        at = pl.ds(pl.multiple_of(i * block, block), block)
        scale = rms(jnp.sum(square_sum(x, at, width), axis=-1, keepdims=True), width)
        qkv[at, :] = (dot(x[at, :], wqkv[...]) * scale).astype(BF16)
        return carry

    lax.fori_loop(0, rows // block, project, 0)

    for a in range(2):
        k = qkv[:, span + a * HD : span + (a + 1) * HD]
        v = qkv[:, 2 * span + a * HD : 2 * span + (a + 1) * HD]
        st[a * per : (a + 1) * per] = dot(k, v, ((0,), (0,))).reshape(per, -1, HD)

    for a in range(2):
        for i in range(rows // block):
            top, end = i * block, (i + 1) * block
            q = qkv[top:end, a * HD : (a + 1) * HD]
            k = qkv[:end, span + a * HD : span + (a + 1) * HD]
            v = qkv[:end, 2 * span + a * HD : 2 * span + (a + 1) * HD]
            scores = dot(q, k, ((1,), (1,)))
            row = lax.broadcasted_iota(jnp.int32, scores.shape, 0) + top
            col = lax.broadcasted_iota(jnp.int32, scores.shape, 1)
            high, low = two_part(jnp.where(row >= col, scores, 0.0))
            att[top:end, a * HD : (a + 1) * HD] = dot(high, v) + dot(low, v)

    ids_r = ids_row[...]
    ids_c = jnp.transpose(jnp.broadcast_to(ids_r.astype(F32), (128, rows)))[:, :1].astype(jnp.int32)
    row = lax.broadcasted_iota(jnp.int32, (rows, rows), 0)
    col = lax.broadcasted_iota(jnp.int32, (rows, rows), 1)
    same = ids_c == ids_r
    rank_r = jnp.sum(jnp.where(same & (row <= col), 1.0, 0.0), axis=0, keepdims=True)
    rank_c = jnp.sum(jnp.where(same & (col <= row), 1.0, 0.0), axis=1, keepdims=True)
    taken = n_seq * CAP
    slots = owned * taken

    def base(ids, rank):
        place = (ids & 1) * taken + (ids >> 1) * CAP
        return place.astype(F32) + (rank - 1.0)

    place = lax.broadcasted_iota(jnp.int32, (slots, 1), 0).astype(F32)
    chosen[...] = jnp.where(place == base(ids_r, rank_r), 1.0, 0.0).astype(BF16)
    place = lax.broadcasted_iota(jnp.int32, (1, slots), 1).astype(F32)
    chosen_t[...] = jnp.where(place == base(ids_c, rank_c), 1.0, 0.0).astype(BF16)

    pl.semaphore_wait(barrier, n_head - 1 + n_seq - 1)
    seq_start(STATE)
    got[s] = st[s]
    def weight_start(i):
        def one(t, carry):
            weight_copy(i, head_peer(t)).start()
            return carry

        lax.fori_loop(1, n_head, one, 0)

    weight_start(0)
    weight_start(1)
    weight_start(2)
    seq_bytes(STATE).wait_recv()

    def running(j, total):
        pre[j] = total
        return total + got[j]

    lax.fori_loop(0, n_seq, running, jnp.zeros(pre.shape[1:], F32))
    seq_start(CARRY)
    car[s] = pre[s]
    weight_bytes(0).wait_recv()
    weight_share(0)

    seq_bytes(CARRY).wait_recv()
    for a in range(2):
        high, low = two_part(car[a * per : (a + 1) * per].reshape(HD, HD))
        q = qkv[:, a * HD : (a + 1) * HD]
        whole = att[:, a * HD : (a + 1) * HD] + dot(q, high) + dot(q, low)
        scale = rms(jnp.sum(whole * whole, axis=-1, keepdims=True), HD)
        hn[h, :, a * HD : (a + 1) * HD] = (whole * scale).astype(BF16)
    gather_start(HEADS)
    gather_start(HEADS + 1)

    loaded(2)
    res[...] = own[...].astype(F32)
    for k in range(2):
        gather_pass(HEADS + k)
    weight_start(5)
    loaded(3)
    weight_bytes(3).wait_recv()

    def use_heads(k, b):
        at = pl.ds(k * middle, middle)
        res[at, :] += dot(hn[b, at, :], wo_v[b])

    for k in range(2):
        use_heads(k, h)
        use_heads(k, partner)
        use_heads(k, left)
        use_heads(k, right)
    for k in range(2):
        gather_far(HEADS + k)
        use_heads(k, far)
        arrived(HEADS + k, TWIN)
        for b in twins:
            use_heads(k, b)
        at = pl.ds(k * middle, middle)
        mid[h, at, :] = res[at, :].astype(BF16)
        gather_start(MIDDLE + k)
        if k == 0:
            for e in range(owned):
                own_lot = pl.ds(e * taken, taken)
                acc[1 + e, pl.ds(0, taken), pl.ds(0, cols)] = dot(chosen[own_lot, at], mid[h, at, :])
    for e in range(owned):
        at = pl.ds(middle, middle)
        picked = acc[1 + e, pl.ds(0, taken), pl.ds(0, cols)] + dot(
            chosen[pl.ds(e * taken, taken), at], mid[h, at, :]
        )
        outb[e] = picked.astype(BF16).reshape(outb.shape[1:])
        seq_send(DISPATCH + 2 * e, 2, n_seq // 2 - 1, 2)
        seq_send(DISPATCH + 2 * e + 1, 1, n_seq // 2, 2)
        rin[h, e, s % 2, s // 2] = outb[e, s]
    weight_bytes(1).wait_recv()
    weight_share(1)

    loaded(6)
    acc[...] = jnp.zeros_like(acc)
    sq[...] = jnp.zeros_like(sq)

    def columns_of(b):
        return pl.ds(pl.multiple_of(b * cols, cols), cols)

    def add_squares(slot, top, part):
        wide = part.astype(F32)
        wide = wide * wide
        total = wide[:, :128]
        for j in range(1, cols // 128):
            total += wide[:, j * 128 : (j + 1) * 128]
        sq[slot, pl.ds(top, part.shape[0]), :] += total

    def use_middle(k, b):
        at = pl.ds(k * middle, middle)
        part = mid[b, at, :]
        acc[0, at, :] += dot(part, sgu[columns_of(b), :])
        add_squares(0, k * middle, part)

    lot_rows = taken // 2

    def use_routed(c, b):
        e, side = lot(c)
        part = rin[b, e, side].reshape(lot_rows, cols)
        acc[1 + e, pl.ds(c % 2 * lot_rows, lot_rows), :] += dot(part, egu[e, columns_of(b), :])
        add_squares(1 + e, c % 2 * lot_rows, part)

    def activate(slot, top, count):
        at = pl.ds(top, count)
        scale = rms(jnp.sum(sq[slot, at, :], axis=-1, keepdims=True), width)
        gate = acc[slot, at, pl.ds(0, hidden)] * scale
        up = acc[slot, at, pl.ds(hidden, hidden)] * scale
        return (silu(gate) * up).astype(BF16)

    near = (left, right)

    def begin(g, use):
        use(h)
        use(partner)
        for b in near:
            use(b)

    def end(g, use):
        use(far)
        arrived(g, TWIN)
        for b in twins:
            use(b)

    def routed(c):
        return functools.partial(use_routed, c)

    def hidden_of(c):
        e, side = lot(c)
        hr[h, e, side] = activate(1 + e, c % 2 * lot_rows, lot_rows)
        gather_start(ROUTED_HIDDEN + c)

    def shared(k):
        return functools.partial(use_middle, k)

    gather_pass(MIDDLE)
    begin(MIDDLE, shared(0))
    gather_pass(MIDDLE + 1)
    seq_bytes(DISPATCH).wait_recv()
    gather_start(ROUTED)
    gather_far(MIDDLE)
    begin(MIDDLE + 1, shared(1))
    seq_bytes(DISPATCH + 1).wait_recv()
    gather_start(ROUTED + 1)
    end(MIDDLE, shared(0))
    gather_far(MIDDLE + 1)
    end(MIDDLE + 1, shared(1))
    hs[h] = activate(0, 0, rows)
    gather_pass(ROUTED)
    seq_bytes(DISPATCH + 2).wait_recv()
    gather_start(ROUTED + 2)
    loaded(7)
    begin(ROUTED, routed(0))
    gather_pass(ROUTED + 1)
    seq_bytes(DISPATCH + 3).wait_recv()
    gather_start(ROUTED + 3)
    gather_far(ROUTED)
    end(ROUTED, routed(0))
    hidden_of(0)
    begin(ROUTED + 1, routed(1))
    gather_pass(ROUTED + 2)
    gather_far(ROUTED + 1)
    end(ROUTED + 1, routed(1))
    hidden_of(1)
    gather_pass(ROUTED_HIDDEN)
    begin(ROUTED + 2, routed(2))
    gather_pass(ROUTED + 3)
    gather_far(ROUTED + 2)
    end(ROUTED + 2, routed(2))
    hidden_of(2)

    loaded(4)
    loaded(5)
    weight_bytes(2).wait_recv()
    weight_bytes(5).wait_recv()

    def use_shared(b):
        res[...] += dot(hs[b], sd_v[b])

    def give_back(c):
        e, side = lot(c)
        total = None
        for b in (h, left, right, far, partner, twin(left), twin(right), twin(far)):
            part = dot(hr[b, e, side], ed_v[b, e])
            total = part if total is None else total + part
        rout[e, side] = total.astype(BF16).reshape(rout.shape[2:])
        if c % 2 == 0:
            seq_send(RETURN + e, 2, n_seq // 2 - 1, 2)
            back[e, s] = rout[e, side, s // 2]
        else:
            seq_send(RETURN + e, 1, n_seq // 2, 2)

    def hidden_end(c):
        arrived(ROUTED_HIDDEN + c, TWIN)

    gather_far(ROUTED_HIDDEN)
    gather_pass(ROUTED_HIDDEN + 1)
    hidden_end(0)
    give_back(0)
    begin(ROUTED + 3, routed(3))
    gather_far(ROUTED + 3)
    end(ROUTED + 3, routed(3))
    hidden_of(3)
    gather_far(ROUTED_HIDDEN + 1)
    gather_pass(ROUTED_HIDDEN + 2)
    hidden_end(1)
    give_back(1)
    gather_far(ROUTED_HIDDEN + 2)
    gather_pass(ROUTED_HIDDEN + 3)
    gather_start(SHARED_HIDDEN)
    hidden_end(2)
    give_back(2)
    gather_far(ROUTED_HIDDEN + 3)
    hidden_end(3)
    give_back(3)

    weight_bytes(4).wait_recv()
    gather_pass(SHARED_HIDDEN)
    gather_far(SHARED_HIDDEN)
    for b in (h, left, right, far):
        use_shared(b)
    use_shared(partner)
    arrived(SHARED_HIDDEN, TWIN)
    for b in twins:
        use_shared(b)
    seq_bytes(RETURN).wait_recv()
    res[...] += dot(chosen_t[:, :taken], back[0].reshape(taken, cols))
    seq_bytes(RETURN + 1).wait_recv()
    final = dot(chosen_t[:, taken:], back[1].reshape(taken, cols))
    out[...] = (res[...] + final).astype(BF16)

    for i in range(6):
        weight_bytes(i).wait_send()
    for e in (STATE, CARRY, DISPATCH, RETURN):
        seq_sent(e)
    for g in (HEADS, MIDDLE, SHARED_HIDDEN, ROUTED, ROUTED_HIDDEN):
        gather_sent(g)


def shards(
    tokens,
    w_query,
    w_key,
    w_value,
    w_out,
    shared_gate,
    shared_up,
    shared_down,
    expert_gate,
    expert_up,
    expert_down,
    expert_ids,
):
    n_seq, n_head = lax.axis_size("seq"), lax.axis_size("head")
    rows, width = tokens.shape
    cols = width // n_head
    owned, _, hidden = expert_gate.shape
    heads = w_query.shape[1]
    taken = n_seq * CAP
    slots = owned * taken
    chunk = heads // n_seq
    most = max(rows, taken)
    any_spec = pl.BlockSpec(memory_space=pl.ANY)
    vmem_spec = pl.BlockSpec(memory_space=pltpu.VMEM)
    V = pltpu.VMEM
    dma = pltpu.SemaphoreType.DMA
    return pl.pallas_call(
        functools.partial(layer_kernel, n_seq, n_head),
        out_shape=jax.ShapeDtypeStruct((rows, cols), BF16),
        in_specs=[any_spec] * 11 + [vmem_spec],
        out_specs=vmem_spec,
        scratch_shapes=[
            V((rows, width), BF16),
            V((rows, cols), BF16),
            V((width, 3 * heads), BF16),
            V((n_head, heads, cols), BF16),
            V((n_head, hidden, cols), BF16),
            V((n_head, owned, hidden, cols), BF16),
            V((width, 2 * hidden), BF16),
            V((owned, width, 2 * hidden), BF16),
            V((rows, 3 * heads), BF16),
            V((n_seq, chunk, HD), F32),
            V((n_seq, chunk, HD), F32),
            V((n_seq, chunk, HD), F32),
            V((n_seq, chunk, HD), F32),
            V((rows, heads), F32),
            V((n_head, rows, heads), BF16),
            V((n_head, rows, cols), BF16),
            V((n_head, owned, 2, n_seq // 2, CAP, cols), BF16),
            V((owned, n_seq, CAP, cols), BF16),
            V((n_head, rows, hidden), BF16),
            V((n_head, owned, 2, taken // 2, hidden), BF16),
            V((owned, 2, n_seq // 2, CAP, cols), BF16),
            V((owned, n_seq, CAP, cols), BF16),
            V((rows, cols), F32),
            V((slots, rows), BF16),
            V((rows, slots), BF16),
            V((1 + owned, most, 2 * hidden), F32),
            V((1 + owned, most, HD), F32),
            dma((8,)),
            dma((6,)),
            dma((6,)),
            dma((4,)),
            dma((EXCHANGES,)),
            dma((5,)),
            dma((GATHERS, 3)),
        ],
        compiler_params=pltpu.CompilerParams(
            collective_id=0, has_side_effects=True, vmem_limit_bytes=60 * 1024 * 1024
        ),
    )(
        tokens, w_query, w_key, w_value, w_out, shared_gate, shared_up, shared_down,
        expert_gate, expert_up, expert_down, expert_ids.reshape(1, rows),
    )


def solution(mesh):
    return jax.shard_map(
        shards,
        mesh=mesh,
        in_specs=(
            P("seq", None),
            P(None, "head"),
            P(None, "head"),
            P(None, "head"),
            P("head", None),
            P(None, "head"),
            P(None, "head"),
            P("head", None),
            P("seq", None, "head"),
            P("seq", None, "head"),
            P("seq", "head", None),
            P("seq", None),
        ),
        out_specs=P("seq", "head"),
        check_vma=False,
    )
```

```python
import functools

import jax
import jax.numpy as jnp
from jax import lax
from jax.experimental import pallas as pl
from jax.experimental.pallas import tpu as pltpu
from jax.sharding import PartitionSpec as P

HD = 128
CAP = 16
NY = 4
F32 = jnp.float32
BF16 = jnp.bfloat16

STATE, CARRY, DISPATCH, RETURN = 0, 1, 2, 6
EXCHANGES = 8
HEADS, MIDDLE, SHARED_HIDDEN, ROUTED, ROUTED_HIDDEN = 0, 2, 4, 5, 9
GATHERS = 13


def dot(a, b, contract=((1,), (0,))):
    return lax.dot_general(a, b, (contract, ((), ())), preferred_element_type=F32)


def two_part(values):
    high = values.astype(BF16)
    return high, (values - high.astype(F32)).astype(BF16)


def rms(total, count):
    return lax.rsqrt(total * (1.0 / count) + 1e-06)


def silu(v):
    return v / (1.0 + jnp.exp(-v))


def layer_kernel(
    n_seq, n_head,
    tok, wq, wk, wv, wo, sg, su, sd, eg, eu, ed, ids_row,
    out,
    x, own, wqkv, wo_v, sd_v, ed_v, sgu, egu, qkv, st, got, pre, car, att,
    hn, mid, rin, outb, hs, hr, rout, back, res, chosen, chosen_t, acc, sq,
    load_sem, w_send, w_recv, s_send, s_recv, g_send, g_recv,
):
    rows, width = x.shape
    cols = width // n_head
    owned = eg.shape[0]
    hidden = eg.shape[2]
    span = 2 * HD
    per = n_seq // 2
    s = lax.axis_index("seq")
    h = lax.axis_index("head")
    core = h % 2
    chip = h // 2
    chips = n_head // 2
    deep = n_seq // NY
    lay = s // deep
    partner = 2 * chip + 1 - core
    right = 2 * ((chip + 1) % chips) + core
    left = 2 * ((chip + chips - 1) % chips) + core
    far = 2 * ((chip + 2) % chips) + core

    def twin(b):
        return 2 * (b // 2) + 1 - b % 2

    def col_slice(index, size):
        return pl.ds(pl.multiple_of(index * size, 128), size)

    def load(i, src, dst):
        return pltpu.make_async_copy(src, dst, load_sem.at[i])

    loads = [
        load(0, tok, x),
        load(1, wq, wqkv.at[:, pl.ds(0, span)]),
        load(1, wk, wqkv.at[:, pl.ds(span, span)]),
        load(1, wv, wqkv.at[:, pl.ds(2 * span, span)]),
        load(2, tok.at[:, col_slice(h, cols)], own),
        load(3, wo.at[:, col_slice(h, cols)], wo_v.at[h]),
        load(4, sd.at[:, col_slice(h, cols)], sd_v.at[h]),
        load(5, ed.at[:, :, col_slice(h, cols)], ed_v.at[h]),
        load(6, sg, sgu.at[:, pl.ds(0, hidden)]),
        load(6, su, sgu.at[:, pl.ds(hidden, hidden)]),
        load(7, eg, egu.at[:, :, pl.ds(0, hidden)]),
        load(7, eu, egu.at[:, :, pl.ds(hidden, hidden)]),
    ]

    def loaded(i):
        ref = (x, wqkv, own, wo_v.at[h], sd_v.at[h], ed_v.at[h], sgu, egu)[i]
        load(i, ref, ref).wait()

    def seq_peer(t):
        return (s + t) % n_seq

    def head_peer(t):
        return (h + t) % n_head

    barrier = pltpu.get_barrier_semaphore()

    def greet_seq(t, carry):
        pl.semaphore_signal(barrier, inc=1, device_id={"seq": seq_peer(t)})
        return carry

    def greet_head(t, carry):
        pl.semaphore_signal(barrier, inc=1, device_id={"head": head_peer(t)})
        return carry

    for copy in loads[:4]:
        copy.start()
    lax.fori_loop(1, n_head, greet_head, 0)
    lax.fori_loop(1, n_seq, greet_seq, 0)
    for copy in loads[4:]:
        copy.start()

    def part_of(i):
        n = (wo_v, sd_v)[i].shape[1] // NY
        return pl.ds(pl.multiple_of(lay * n, n), n)

    def ed_lines(i):
        early = hidden // 4 * 3
        return pl.ds(0, early) if i == 2 else pl.ds(early, hidden - early)

    def weight_copy(i, peer):
        at = col_slice(peer, cols)
        if i in (2, 5):
            lines = ed_lines(i)
            src, dst = ed.at[:, lines, at], ed_v.at[h, :, lines]
        else:
            src, dst = (wo, sd)[i].at[part_of(i), at], (wo_v, sd_v)[i].at[h, part_of(i)]
        return pltpu.make_async_remote_copy(
            src, dst, w_send.at[i], w_recv.at[i], device_id={"head": peer}
        )

    def weight_bytes(i):
        some = pl.ds(0, n_head - 1)
        if i in (2, 5):
            ref = ed_v.at[some, :, ed_lines(i)]
        elif i < 2:
            ref = (wo_v, sd_v)[i].at[some, pl.ds(0, (wo_v, sd_v)[i].shape[1] // NY)]
        else:
            whole = (wo_v, sd_v)[i - 3]
            ref = whole.at[some, pl.ds(0, whole.shape[1] // NY * (NY - 1))]
        return pltpu.make_async_remote_copy(
            ref, ref, w_send.at[i], w_recv.at[i], device_id={"head": partner}
        )

    def weight_share(i, first=1, end=None):
        whole = (wo_v, sd_v)[i]

        def one(t, carry):
            ref = whole.at[head_peer(t), part_of(i)]
            for k in (2, 1, 3):
                pltpu.make_async_remote_copy(
                    ref, ref, w_send.at[3 + i], w_recv.at[3 + i],
                    device_id={"seq": ((lay + k) % NY) * deep + s % deep},
                ).start()
            return carry

        lax.fori_loop(first, end or n_head, one, 0)

    def seq_refs(e, peer):
        if e == STATE:
            return st.at[peer], got.at[s]
        if e == CARRY:
            return pre.at[peer], car.at[s]
        if e >= RETURN:
            return rout.at[e - RETURN, peer % 2, peer // 2], back.at[e - RETURN, s]
        e = (e - DISPATCH) // 2
        return outb.at[e, peer], rin.at[h, e, s % 2, s // 2]

    def source_of(e):
        return min(e, DISPATCH) + (e >= RETURN)

    def seq_send(e, first, last, stride):
        def one(t, carry):
            peer = seq_peer(t * stride + first)
            src, dst = seq_refs(e, peer)
            pltpu.make_async_remote_copy(
                src, dst, s_send.at[source_of(e)], s_recv.at[e], device_id={"seq": peer}
            ).start()
            return carry

        lax.fori_loop(0, last, one, 0)

    def seq_start(e):
        seq_send(e, 1, n_seq - 1, 1)

    def seq_bytes(e):
        ref = st if e == STATE else pre if e == CARRY else back.at[0]
        count = n_seq - 1
        if DISPATCH <= e < RETURN:
            count = n_seq // 2 - 1 + e % 2
        ref = ref.at[pl.ds(0, count)]
        return pltpu.make_async_remote_copy(
            ref, ref, s_send.at[source_of(e)], s_recv.at[e], device_id={"seq": seq_peer(1)}
        )

    def seq_sent(e):
        some = pl.ds(0, n_seq - 1)
        ref = st if e == STATE else pre if e == CARRY else back
        ref = ref.at[some] if e < DISPATCH else ref.at[:, some]
        pltpu.make_async_remote_copy(
            ref, ref, s_send.at[source_of(e)], s_recv.at[e], device_id={"seq": seq_peer(1)}
        ).wait_send()

    parity = s % 2
    middle = rows // 2

    def lot(c):
        return c // 2, (parity + c) % 2

    def view(g, b):
        if g < SHARED_HIDDEN:
            ref = hn if g < MIDDLE else mid
            return ref.at[b, pl.ds(g % 2 * middle, middle)]
        if g == SHARED_HIDDEN:
            return hs.at[b]
        e, side = lot((g - ROUTED) % 4)
        return (rin if g < ROUTED_HIDDEN else hr).at[b, e, side]

    def half(g, b, k):
        whole = view(g, b)
        n = whole.shape[0] // 2
        return whole.at[pl.ds(k * n, n)]

    def buffer_of(g):
        return (g >= MIDDLE) + (g >= SHARED_HIDDEN) + (g >= ROUTED) + (g >= ROUTED_HIDDEN)

    def leg(g, ref, i, target):
        return pltpu.make_async_remote_copy(
            ref, ref, g_send.at[buffer_of(g)], g_recv.at[g, i], device_id={"head": target}
        )

    NEAR, FAR, TWIN = range(3)

    def arrived(g, i):
        count = (3, 1, 3)[i]
        leg(g, view(g, pl.ds(0, count)), i, partner).wait_recv()

    twins = (twin(left), twin(right), twin(far))

    def gather_start(g):
        for target in (right, left, partner):
            leg(g, view(g, h), NEAR, target).start()

    def gather_pass(g):
        arrived(g, NEAR)
        leg(g, half(g, left, 0), FAR, right).start()
        leg(g, half(g, right, 1), FAR, left).start()
        leg(g, view(g, left), TWIN, partner).start()
        leg(g, view(g, right), TWIN, partner).start()

    def gather_far(g):
        arrived(g, FAR)
        leg(g, view(g, far), TWIN, partner).start()

    def gather_sent(g):
        ref = (hn, mid, hs, rin, hr)[buffer_of(g)].at[pl.ds(0, n_head - 1)]
        leg(g, ref, 0, partner).wait_send()

    loaded(0)
    loaded(1)
    block = min(256, rows)

    def square_sum(ref, at, count):
        total = None
        for j in range(count // 128):
            wide = ref[at, j * 128 : (j + 1) * 128].astype(F32)
            total = wide * wide if total is None else total + wide * wide
        return total

    def project(i, carry):
        at = pl.ds(pl.multiple_of(i * block, block), block)
        scale = rms(jnp.sum(square_sum(x, at, width), axis=-1, keepdims=True), width)
        qkv[at, :] = (dot(x[at, :], wqkv[...]) * scale).astype(BF16)
        return carry

    lax.fori_loop(0, rows // block, project, 0)

    for a in range(2):
        k = qkv[:, span + a * HD : span + (a + 1) * HD]
        v = qkv[:, 2 * span + a * HD : 2 * span + (a + 1) * HD]
        st[a * per : (a + 1) * per] = dot(k, v, ((0,), (0,))).reshape(per, -1, HD)

    for a in range(2):
        for i in range(rows // block):
            top, end = i * block, (i + 1) * block
            q = qkv[top:end, a * HD : (a + 1) * HD]
            k = qkv[:end, span + a * HD : span + (a + 1) * HD]
            v = qkv[:end, 2 * span + a * HD : 2 * span + (a + 1) * HD]
            scores = dot(q, k, ((1,), (1,)))
            row = lax.broadcasted_iota(jnp.int32, scores.shape, 0) + top
            col = lax.broadcasted_iota(jnp.int32, scores.shape, 1)
            high, low = two_part(jnp.where(row >= col, scores, 0.0))
            att[top:end, a * HD : (a + 1) * HD] = dot(high, v) + dot(low, v)

    ids_r = ids_row[...]
    ids_c = jnp.transpose(jnp.broadcast_to(ids_r.astype(F32), (128, rows)))[:, :1].astype(jnp.int32)
    row = lax.broadcasted_iota(jnp.int32, (rows, rows), 0)
    col = lax.broadcasted_iota(jnp.int32, (rows, rows), 1)
    same = ids_c == ids_r
    rank_r = jnp.sum(jnp.where(same & (row <= col), 1.0, 0.0), axis=0, keepdims=True)
    rank_c = jnp.sum(jnp.where(same & (col <= row), 1.0, 0.0), axis=1, keepdims=True)
    taken = n_seq * CAP
    slots = owned * taken

    def base(ids, rank):
        place = (ids & 1) * taken + (ids >> 1) * CAP
        return place.astype(F32) + (rank - 1.0)

    place = lax.broadcasted_iota(jnp.int32, (slots, 1), 0).astype(F32)
    chosen[...] = jnp.where(place == base(ids_r, rank_r), 1.0, 0.0).astype(BF16)
    place = lax.broadcasted_iota(jnp.int32, (1, slots), 1).astype(F32)
    chosen_t[...] = jnp.where(place == base(ids_c, rank_c), 1.0, 0.0).astype(BF16)

    pl.semaphore_wait(barrier, n_head - 1 + n_seq - 1)
    seq_start(STATE)
    got[s] = st[s]
    def weight_start(i):
        def one(t, carry):
            weight_copy(i, head_peer(t)).start()
            return carry

        lax.fori_loop(1, n_head, one, 0)

    weight_start(0)
    weight_start(1)
    weight_start(2)
    seq_bytes(STATE).wait_recv()

    def running(j, total):
        pre[j] = total
        return total + got[j]

    lax.fori_loop(0, n_seq, running, jnp.zeros(pre.shape[1:], F32))
    seq_start(CARRY)
    car[s] = pre[s]
    weight_bytes(0).wait_recv()
    weight_share(0)

    seq_bytes(CARRY).wait_recv()
    for a in range(2):
        high, low = two_part(car[a * per : (a + 1) * per].reshape(HD, HD))
        q = qkv[:, a * HD : (a + 1) * HD]
        whole = att[:, a * HD : (a + 1) * HD] + dot(q, high) + dot(q, low)
        scale = rms(jnp.sum(whole * whole, axis=-1, keepdims=True), HD)
        hn[h, :, a * HD : (a + 1) * HD] = (whole * scale).astype(BF16)
    gather_start(HEADS)
    gather_start(HEADS + 1)

    loaded(2)
    res[...] = own[...].astype(F32)
    for k in range(2):
        gather_pass(HEADS + k)
    weight_start(5)
    loaded(3)
    weight_bytes(3).wait_recv()

    def use_heads(k, b):
        at = pl.ds(k * middle, middle)
        res[at, :] += dot(hn[b, at, :], wo_v[b])

    for k in range(2):
        use_heads(k, h)
        use_heads(k, partner)
        use_heads(k, left)
        use_heads(k, right)
    for k in range(2):
        gather_far(HEADS + k)
        use_heads(k, far)
        arrived(HEADS + k, TWIN)
        for b in twins:
            use_heads(k, b)
        at = pl.ds(k * middle, middle)
        mid[h, at, :] = res[at, :].astype(BF16)
        gather_start(MIDDLE + k)
        if k == 0:
            for e in range(owned):
                own_lot = pl.ds(e * taken, taken)
                acc[1 + e, pl.ds(0, taken), pl.ds(0, cols)] = dot(chosen[own_lot, at], mid[h, at, :])
    for e in range(owned):
        at = pl.ds(middle, middle)
        picked = acc[1 + e, pl.ds(0, taken), pl.ds(0, cols)] + dot(
            chosen[pl.ds(e * taken, taken), at], mid[h, at, :]
        )
        outb[e] = picked.astype(BF16).reshape(outb.shape[1:])
        seq_send(DISPATCH + 2 * e, 2, n_seq // 2 - 1, 2)
        seq_send(DISPATCH + 2 * e + 1, 1, n_seq // 2, 2)
        rin[h, e, s % 2, s // 2] = outb[e, s]
    weight_bytes(1).wait_recv()
    weight_share(1)

    loaded(6)
    acc[...] = jnp.zeros_like(acc)
    sq[...] = jnp.zeros_like(sq)

    def columns_of(b):
        return pl.ds(pl.multiple_of(b * cols, cols), cols)

    def add_squares(slot, top, part):
        wide = part.astype(F32)
        wide = wide * wide
        total = wide[:, :128]
        for j in range(1, cols // 128):
            total += wide[:, j * 128 : (j + 1) * 128]
        sq[slot, pl.ds(top, part.shape[0]), :] += total

    def use_middle(k, b):
        at = pl.ds(k * middle, middle)
        part = mid[b, at, :]
        acc[0, at, :] += dot(part, sgu[columns_of(b), :])
        add_squares(0, k * middle, part)

    lot_rows = taken // 2

    def use_routed(c, b):
        e, side = lot(c)
        part = rin[b, e, side].reshape(lot_rows, cols)
        acc[1 + e, pl.ds(c % 2 * lot_rows, lot_rows), :] += dot(part, egu[e, columns_of(b), :])
        add_squares(1 + e, c % 2 * lot_rows, part)

    def activate(slot, top, count):
        at = pl.ds(top, count)
        scale = rms(jnp.sum(sq[slot, at, :], axis=-1, keepdims=True), width)
        gate = acc[slot, at, pl.ds(0, hidden)] * scale
        up = acc[slot, at, pl.ds(hidden, hidden)] * scale
        return (silu(gate) * up).astype(BF16)

    near = (left, right)

    def begin(g, use):
        use(h)
        use(partner)
        for b in near:
            use(b)

    def end(g, use):
        use(far)
        arrived(g, TWIN)
        for b in twins:
            use(b)

    def routed(c):
        return functools.partial(use_routed, c)

    def hidden_of(c):
        e, side = lot(c)
        hr[h, e, side] = activate(1 + e, c % 2 * lot_rows, lot_rows)
        gather_start(ROUTED_HIDDEN + c)

    def shared(k):
        return functools.partial(use_middle, k)

    gather_pass(MIDDLE)
    begin(MIDDLE, shared(0))
    gather_pass(MIDDLE + 1)
    seq_bytes(DISPATCH).wait_recv()
    gather_start(ROUTED)
    gather_far(MIDDLE)
    begin(MIDDLE + 1, shared(1))
    seq_bytes(DISPATCH + 1).wait_recv()
    gather_start(ROUTED + 1)
    end(MIDDLE, shared(0))
    gather_far(MIDDLE + 1)
    end(MIDDLE + 1, shared(1))
    hs[h] = activate(0, 0, rows)
    gather_pass(ROUTED)
    seq_bytes(DISPATCH + 2).wait_recv()
    gather_start(ROUTED + 2)
    loaded(7)
    begin(ROUTED, routed(0))
    gather_pass(ROUTED + 1)
    seq_bytes(DISPATCH + 3).wait_recv()
    gather_start(ROUTED + 3)
    gather_far(ROUTED)
    end(ROUTED, routed(0))
    hidden_of(0)
    begin(ROUTED + 1, routed(1))
    gather_pass(ROUTED + 2)
    gather_far(ROUTED + 1)
    end(ROUTED + 1, routed(1))
    hidden_of(1)
    gather_pass(ROUTED_HIDDEN)
    begin(ROUTED + 2, routed(2))
    gather_pass(ROUTED + 3)
    gather_far(ROUTED + 2)
    end(ROUTED + 2, routed(2))
    hidden_of(2)

    loaded(4)
    loaded(5)
    weight_bytes(2).wait_recv()
    weight_bytes(5).wait_recv()

    def use_shared(b):
        res[...] += dot(hs[b], sd_v[b])

    def give_back(c):
        e, side = lot(c)
        total = None
        for b in (h, left, right, far, partner, twin(left), twin(right), twin(far)):
            part = dot(hr[b, e, side], ed_v[b, e])
            total = part if total is None else total + part
        rout[e, side] = total.astype(BF16).reshape(rout.shape[2:])
        if c % 2 == 0:
            seq_send(RETURN + e, 2, n_seq // 2 - 1, 2)
            back[e, s] = rout[e, side, s // 2]
        else:
            seq_send(RETURN + e, 1, n_seq // 2, 2)

    def hidden_end(c):
        arrived(ROUTED_HIDDEN + c, TWIN)

    gather_far(ROUTED_HIDDEN)
    gather_pass(ROUTED_HIDDEN + 1)
    hidden_end(0)
    give_back(0)
    begin(ROUTED + 3, routed(3))
    gather_far(ROUTED + 3)
    end(ROUTED + 3, routed(3))
    hidden_of(3)
    gather_far(ROUTED_HIDDEN + 1)
    gather_pass(ROUTED_HIDDEN + 2)
    hidden_end(1)
    give_back(1)
    gather_far(ROUTED_HIDDEN + 2)
    gather_pass(ROUTED_HIDDEN + 3)
    gather_start(SHARED_HIDDEN)
    hidden_end(2)
    give_back(2)
    gather_far(ROUTED_HIDDEN + 3)
    hidden_end(3)
    give_back(3)

    weight_bytes(4).wait_recv()
    gather_pass(SHARED_HIDDEN)
    for b in (h, partner, left, right):
        use_shared(b)
    gather_far(SHARED_HIDDEN)
    use_shared(far)
    seq_bytes(RETURN).wait_recv()
    res[...] += dot(chosen_t[:, :taken], back[0].reshape(taken, cols))
    arrived(SHARED_HIDDEN, TWIN)
    for b in twins:
        use_shared(b)
    seq_bytes(RETURN + 1).wait_recv()
    final = dot(chosen_t[:, taken:], back[1].reshape(taken, cols))
    out[...] = (res[...] + final).astype(BF16)

    for i in range(6):
        weight_bytes(i).wait_send()
    for e in (STATE, CARRY, DISPATCH, RETURN):
        seq_sent(e)
    for g in (HEADS, MIDDLE, SHARED_HIDDEN, ROUTED, ROUTED_HIDDEN):
        gather_sent(g)


def shards(
    tokens,
    w_query,
    w_key,
    w_value,
    w_out,
    shared_gate,
    shared_up,
    shared_down,
    expert_gate,
    expert_up,
    expert_down,
    expert_ids,
):
    n_seq, n_head = lax.axis_size("seq"), lax.axis_size("head")
    rows, width = tokens.shape
    cols = width // n_head
    owned, _, hidden = expert_gate.shape
    heads = w_query.shape[1]
    taken = n_seq * CAP
    slots = owned * taken
    chunk = heads // n_seq
    most = max(rows, taken)
    any_spec = pl.BlockSpec(memory_space=pl.ANY)
    vmem_spec = pl.BlockSpec(memory_space=pltpu.VMEM)
    V = pltpu.VMEM
    dma = pltpu.SemaphoreType.DMA
    return pl.pallas_call(
        functools.partial(layer_kernel, n_seq, n_head),
        out_shape=jax.ShapeDtypeStruct((rows, cols), BF16),
        in_specs=[any_spec] * 11 + [vmem_spec],
        out_specs=vmem_spec,
        scratch_shapes=[
            V((rows, width), BF16),
            V((rows, cols), BF16),
            V((width, 3 * heads), BF16),
            V((n_head, heads, cols), BF16),
            V((n_head, hidden, cols), BF16),
            V((n_head, owned, hidden, cols), BF16),
            V((width, 2 * hidden), BF16),
            V((owned, width, 2 * hidden), BF16),
            V((rows, 3 * heads), BF16),
            V((n_seq, chunk, HD), F32),
            V((n_seq, chunk, HD), F32),
            V((n_seq, chunk, HD), F32),
            V((n_seq, chunk, HD), F32),
            V((rows, heads), F32),
            V((n_head, rows, heads), BF16),
            V((n_head, rows, cols), BF16),
            V((n_head, owned, 2, n_seq // 2, CAP, cols), BF16),
            V((owned, n_seq, CAP, cols), BF16),
            V((n_head, rows, hidden), BF16),
            V((n_head, owned, 2, taken // 2, hidden), BF16),
            V((owned, 2, n_seq // 2, CAP, cols), BF16),
            V((owned, n_seq, CAP, cols), BF16),
            V((rows, cols), F32),
            V((slots, rows), BF16),
            V((rows, slots), BF16),
            V((1 + owned, most, 2 * hidden), F32),
            V((1 + owned, most, HD), F32),
            dma((8,)),
            dma((6,)),
            dma((6,)),
            dma((4,)),
            dma((EXCHANGES,)),
            dma((5,)),
            dma((GATHERS, 3)),
        ],
        compiler_params=pltpu.CompilerParams(
            collective_id=0, has_side_effects=True, vmem_limit_bytes=60 * 1024 * 1024
        ),
    )(
        tokens, w_query, w_key, w_value, w_out, shared_gate, shared_up, shared_down,
        expert_gate, expert_up, expert_down, expert_ids.reshape(1, rows),
    )


def solution(mesh):
    return jax.shard_map(
        shards,
        mesh=mesh,
        in_specs=(
            P("seq", None),
            P(None, "head"),
            P(None, "head"),
            P(None, "head"),
            P("head", None),
            P(None, "head"),
            P(None, "head"),
            P("head", None),
            P("seq", None, "head"),
            P("seq", None, "head"),
            P("seq", "head", None),
            P("seq", None),
        ),
        out_specs=P("seq", "head"),
        check_vma=False,
    )
```
